512 devices in a mesh: tm: 16 (over y_lo, x, core), sx: 8 (over z), sy: 4 (over y_hi).
Axes of the slice: x: 4, y: 8 (y_hi: 4, y_lo: 2; y = y_hi * 2 + y_lo), z: 8, core: 2. Of those that a mesh axis runs over, the one named last changes fastest.
Arguments:
- initial: float32 [2048, 2048], P('sx', 'sy'), may hold values from 0.5 to 1.5
- kappa: float32 [2048, 2048], P('sx', 'sy'), may hold values from 0.0016 to 0.016
- c_guess: float32 [16, 2048, 2048], P('tm', 'sx', 'sy'), may hold values from 0.5 to 1.5
Outputs:
- c_values: float32 [16, 2048, 2048], P('tm', 'sx', 'sy')
- f_values: float32 [16, 2048, 2048], P('tm', 'sx', 'sy')
The draws below stay inside these ranges and needn't reach their ends.
All inputs are finite; a program needn't handle non-finite values.
Results may differ from the reference program's by a relative error of at most 0.00002.
Values sent between devices are 32-bit elements; how exact they have to be, the bound alone decides.
A program may use at most 64 MiB of HBM per device.

```python
import math
import jax
import jax.numpy as jnp

NT1 = 16
NT2 = 8
NX = 2048
NY = 2048


def shard_levels(stream_key, extent, split, least, high):
    gain = 1.0
    for dim, shards_of in split:
        draws = jax.random.uniform(jax.random.fold_in(jax.random.fold_in(stream_key, 6), dim), (shards_of,), jnp.float32, least / len(split), high / len(split))
        gain = gain * jnp.repeat(jnp.exp(draws), extent[dim] // shards_of).reshape((-1,) + (1,) * (len(extent) - 1 - dim))
    return gain


def setup_inputs(seed: int = 0) -> dict:
    key_list = jax.random.split(jax.random.key(seed), 4)
    initial = jnp.clip(0.5 + 1.0 * jax.random.uniform(key_list[0], (NX, NY), jnp.float32) ** shard_levels(key_list[0], (NX, NY), ((0, 8), (1, 4)), -0.2, 0.2), 0.5, 1.5)
    kappa = jnp.clip(jnp.exp(math.log(0.016) - 2.3025852 * jax.random.uniform(key_list[1], (NX, NY), jnp.float32) ** shard_levels(key_list[1], (NX, NY), ((0, 8), (1, 4)), -0.2, 0.2)), 0.0016, 0.016)
    c_guess = jnp.clip(0.5 + 1.0 * jax.random.uniform(key_list[2], (NT1, NX, NY), jnp.float32) ** shard_levels(key_list[2], (NT1, NX, NY), ((0, 16), (1, 8), (2, 4)), -0.2, 0.2), 0.5, 1.5)
    return dict(initial=initial, kappa=kappa, c_guess=c_guess)


def spread(field, kappa):
    flux = kappa * field * field
    widths = [(0, 0)] * (flux.ndim - 2) + [(1, 1), (1, 1)]
    padded = jnp.pad(flux, widths)
    return padded[..., 2:, 1:-1] + padded[..., :-2, 1:-1] + padded[..., 1:-1, 2:] + padded[..., 1:-1, :-2] - 4.0 * flux


def reference(initial, kappa, c_guess):
    prev_w = jnp.concatenate([initial[None], c_guess[:-1]], axis=0)
    lap_w = spread(prev_w, kappa)
    fine = prev_w + lap_w
    lap_f = spread(fine, kappa)
    value = fine + lap_f
    first_rhs = value - prev_w - 2.0 * lap_w
    quarter = prev_w + 4.0 * lap_w
    value_odd = value[0::2]
    second_rhs = value_odd + 2.0 * spread(value_odd, kappa) + first_rhs[1::2] - quarter[0::2]
    state = initial
    states = [initial]
    for level in range(NT2):
        state = state + 4.0 * spread(state, kappa) + second_rhs[level]
        states.append(state)
    coarse = jnp.stack(states)
    lower = coarse[:-1]
    even_part = lower + 2.0 * spread(lower, kappa) + first_rhs[0::2]
    odd_part = coarse[1:]
    c_values = jnp.stack([even_part, odd_part], axis=1).reshape(NT1, NX, NY)
    prev_n = jnp.concatenate([initial[None], c_values[:-1]], axis=0)
    f_values = prev_n + spread(prev_n, kappa)
    return c_values, f_values
```

```python
import jax
import jax.numpy as jnp
from jax import lax
from jax.experimental import pallas as pl
from jax.experimental.pallas import tpu as pltpu
from jax.sharding import PartitionSpec as P

MESH = pl.DeviceIdType.MESH
F32 = jnp.float32
ROWS, COLS = 256, 512
EXT, WIDE = ROWS + 32, COLS + 128
CHIPS = 8
WIN = 64
BLOCK = 48


def lap(v, kap):
    a = kap * v * v
    r, w = a.shape
    around = pltpu.roll(a, 1, 0) + pltpu.roll(a, r - 1, 0) + pltpu.roll(a, 1, 1) + pltpu.roll(a, w - 1, 1)
    return around - 4.0 * a


def first_part(p, kap):
    lap_p = lap(p, kap)
    f = p + lap_p
    v = f + lap(f, kap)
    return v - p - 2.0 * lap_p


def second_part(p, kap):
    lap_p = lap(p, kap)
    f = p + lap_p
    v = f + lap(f, kap)
    return v + 2.0 * lap(v, kap) - (p + 4.0 * lap_p)


def pack(x, back):
    x = x.reshape(4, 8, 8, 128)
    lane = lax.broadcasted_iota(jnp.int32, (4, 8, 128), 2)
    out = jnp.zeros((4, 8, 128), F32)
    for b in range(8):
        shift = (16 * b + back) % 128
        part = pltpu.roll(x[:, b], shift, 2) if shift else x[:, b]
        out = jnp.where((lane >= 16 * b) & (lane < 16 * b + 16), part, out)
    return out.reshape(32, 128)


def unpack(right, left):
    right, left = right.reshape(4, 8, 128), left.reshape(4, 8, 128)
    lane = lax.broadcasted_iota(jnp.int32, (4, 8, 128), 2)
    parts = []
    for b in range(8):
        r = pltpu.roll(right, (128 - 16 * b) % 128, 2) if b else right
        s = (112 - 16 * b) % 128
        l = pltpu.roll(left, s, 2) if s else left
        parts.append(jnp.where(lane < 16, r, jnp.where(lane >= 112, l, 0.0)))
    return jnp.stack(parts, axis=1).reshape(ROWS, 128)


def kernel(
    init_hbm, kap_hbm, guess_hbm, c_out, f_out,
    ie, ke, ce, strips, strips_in, got, us, ur, xs, xb, sh, eb, ga, gb,
    ld, st_s, st_r, row_s, row_r, a_s, a_r, h_s, h_r, e_s, e_r, own, sh_s, sh_r, shf_s, shf_r, eb_s, eb_r,
    u_s, u_r, x_s, x_r, xe_s, xe_r, xl, xf_s, xf_r,
):
    t, sx, sy = lax.axis_index("tm"), lax.axis_index("sx"), lax.axis_index("sy")
    nx, ny = lax.axis_size("sx"), lax.axis_size("sy")
    c, p = t // 2, lax.rem(t, 2)
    even, odd = p == 0, p == 1
    up, down = lax.rem(sx + nx - 1, nx), lax.rem(sx + 1, nx)
    left, right = lax.rem(sy + ny - 1, ny), lax.rem(sy + 1, ny)
    partner = t + 1 - 2 * p
    fields = (ie, ke, ce)

    loads = [
        pltpu.make_async_copy(src, dst.at[16 : 16 + ROWS, 0:COLS], ld.at[n])
        for n, (src, dst) in enumerate(((init_hbm, ie), (kap_hbm, ke), (guess_hbm.at[0], ce)))
    ]
    for cp in loads:
        cp.start()
    got[...] = jnp.zeros(got.shape, F32)

    barrier = pltpu.get_barrier_semaphore()

    def greet(d, carry):
        pl.semaphore_signal(barrier, inc=1, device_id={"tm": 2 * lax.rem(c + d, CHIPS) + p}, device_id_type=MESH)
        return carry

    lax.fori_loop(1, CHIPS, greet, 0)
    for there in ({"tm": partner}, {"sx": up}, {"sx": down}, {"sy": left}, {"sy": right}):
        pl.semaphore_signal(barrier, inc=1, device_id=there, device_id_type=MESH)
    pl.semaphore_wait(barrier, CHIPS - 1 + 5)

    def remote(src, dst, s, r, there):
        return pltpu.make_async_remote_copy(src, dst, s, r, device_id=there, device_id_type=MESH)

    def main_copy(i, slot):
        start = jnp.clip(32 * i - 8, 0, ROWS - BLOCK)
        src = ce.at[pl.ds(pl.multiple_of(start + 16, 8), BLOCK), 0:COLS]
        dst = got.at[slot, pl.ds(pl.multiple_of(start + 16 - 32 * i, 8), BLOCK), 0:COLS]
        return remote(src, dst, a_s.at[i], a_r.at[slot], {"tm": 2 * i + p})

    def side_copy(i, slot):
        start = jnp.clip(32 * i - 8, 0, ROWS - BLOCK)
        src = ce.at[pl.ds(pl.multiple_of(start + 16, 8), BLOCK), COLS:WIDE]
        dst = got.at[slot, pl.ds(pl.multiple_of(start + 16 - 32 * i, 8), BLOCK), COLS:WIDE]
        return remote(src, dst, h_s.at[i], h_r.at[slot], {"tm": 2 * i + p})

    def top_copy(slot):
        return remote(ce.at[0:16], got.at[slot, 0:16], e_s.at[0], e_r.at[slot], {"tm": p})

    def bottom_copy(slot):
        return remote(ce.at[EXT - 16 : EXT], got.at[slot, 48:64], e_s.at[1], e_r.at[slot], {"tm": 2 * CHIPS - 2 + p})

    loads[2].wait()
    sends_guess = t <= 12

    @pl.when(sends_guess)
    def _():
        def send(d, carry):
            main_copy(lax.rem(c + d, CHIPS), c).start()
            return carry

        lax.fori_loop(1, CHIPS, send, 0)

    loads[0].wait()
    loads[1].wait()
    for n, ref in enumerate(fields):
        strips[0, 32 * n : 32 * n + 32] = pack(ref[16 : 16 + ROWS, 0:128], 0)
        strips[1, 32 * n : 32 * n + 32] = pack(ref[16 : 16 + ROWS, COLS - 128 : COLS], 16)
    side = [
        remote(strips.at[0], strips_in.at[0], st_s.at[0], st_r.at[0], {"sy": left}),
        remote(strips.at[1], strips_in.at[1], st_s.at[1], st_r.at[1], {"sy": right}),
    ]
    for cp in side:
        cp.start()
    for cp in side:
        cp.wait_recv()
    keep_right = jnp.where(sy == ny - 1, 0.0, 1.0).astype(F32)
    keep_left = jnp.where(sy == 0, 0.0, 1.0).astype(F32)
    for n, ref in enumerate(fields):
        r, l = strips_in[0, 32 * n : 32 * n + 32], strips_in[1, 32 * n : 32 * n + 32]
        if n == 1:
            r, l = r * keep_right, l * keep_left
        ref[16 : 16 + ROWS, COLS:WIDE] = unpack(r, l)

    rows = []
    for n, ref in enumerate(fields):
        rows.append(remote(ref.at[16:32], ref.at[EXT - 16 : EXT], row_s.at[2 * n], row_r.at[2 * n], {"sx": up}))
        rows.append(remote(ref.at[EXT - 32 : EXT - 16], ref.at[0:16], row_s.at[2 * n + 1], row_r.at[2 * n + 1], {"sx": down}))
    for cp in rows:
        cp.start()

    @pl.when(sends_guess)
    def _():
        def send(d, carry):
            side_copy(lax.rem(c + d, CHIPS), c).start()
            return carry

        lax.fori_loop(1, CHIPS, send, 0)

    for cp in rows:
        cp.wait_recv()

    @pl.when(sends_guess & (c != 0))
    def _():
        top_copy(c).start()

    @pl.when(sends_guess & (c != CHIPS - 1))
    def _():
        bottom_copy(c).start()

    @pl.when(sx == 0)
    def _():
        ke[0:16] = jnp.zeros((16, WIDE), F32)

    @pl.when(sx == nx - 1)
    def _():
        ke[EXT - 16 : EXT] = jnp.zeros((16, WIDE), F32)

    shift = remote(ce.at[8 : EXT - 8], sh.at[8 : EXT - 8], sh_s, sh_r, {"tm": jnp.minimum(t + 2, 2 * CHIPS - 1)})
    pass_on = remote(sh.at[8 : EXT - 8], sh.at[8 : EXT - 8], shf_s, shf_r, {"tm": partner})
    own_even = remote(ce.at[8 : EXT - 8], eb.at[8 : EXT - 8], eb_s, eb_r, {"tm": partner})
    first_sh = pltpu.make_async_copy(ie.at[8 : EXT - 8], sh.at[8 : EXT - 8], own.at[1])

    @pl.when(odd & (c < CHIPS - 1))
    def _():
        shift.start()

    @pl.when(even)
    def _():
        own_even.start()

    @pl.when(c == 0)
    def _():
        first_sh.start()

    at = pl.multiple_of(32 * c, 32)
    mine = pltpu.make_async_copy(ce.at[pl.ds(at, WIN)], got.at[c], own.at[0])

    @pl.when(sends_guess)
    def _():
        mine.start()

    def arrive(m):
        @pl.when(m == c)
        def _():
            mine.wait()

        @pl.when(m != c)
        def _():
            main_copy(c, m).wait_recv()
            side_copy(c, m).wait_recv()

            @pl.when(c == 0)
            def _():
                top_copy(m).wait_recv()

            @pl.when(c == CHIPS - 1)
            def _():
                bottom_copy(m).wait_recv()

    def u_copy(m):
        return remote(us.at[m], ur.at[m + 1], u_s.at[m], u_r.at[m], {"tm": partner})

    def x_copy(i, j):
        dst = xb.at[pl.ds(pl.multiple_of(32 * i + 16, 8), 32)]
        return remote(xs.at[j, 16:48], dst, x_s.at[j], x_r.at[i], {"tm": 2 * j})

    def x_local(j):
        dst = xb.at[pl.ds(pl.multiple_of(32 * c + 16, 8), 32)]
        return pltpu.make_async_copy(xs.at[j, 16:48], dst, xl.at[0])

    def xe_copy(top, j):
        if top:
            return remote(xs.at[j, 8:16], xb.at[8:16], xe_s.at[j], xe_r.at[0], {"tm": 2 * j})
        return remote(xs.at[j, 48:56], xb.at[EXT - 16 : EXT - 8], xe_s.at[j], xe_r.at[1], {"tm": 2 * j})

    def xe_local(top, j):
        if top:
            return pltpu.make_async_copy(xs.at[j, 8:16], xb.at[8:16], xl.at[1])
        return pltpu.make_async_copy(xs.at[j, 48:56], xb.at[EXT - 16 : EXT - 8], xl.at[1])

    @pl.when(odd)
    def _():
        def point(m, carry):
            arrive(m)
            us[m] = second_part(got[m], ke[pl.ds(at, WIN)])
            u_copy(m).start()
            return carry

        lax.fori_loop(0, 6, point, 0)

    @pl.when(even)
    def _():
        ur[0] = second_part(ie[pl.ds(at, WIN)], ke[pl.ds(at, WIN)])
        xs[0] = ie[pl.ds(at, WIN)]

        def point(j, carry):
            kap = ke[pl.ds(at, WIN)]
            arrive(j - 1)
            part = first_part(got[j - 1], kap)

            @pl.when(j > 1)
            def _():
                u_copy(jnp.maximum(j - 2, 0)).wait_recv()

            x = xs[j - 1]
            xs[j] = x + 4.0 * lap(x, kap) + (ur[j - 1] + part)

            @pl.when(j != c)
            def _():
                x_copy(c, j).start()

                @pl.when(c == 0)
                def _():
                    xe_copy(True, j).start()

                @pl.when(c == CHIPS - 1)
                def _():
                    xe_copy(False, j).start()

            @pl.when(j == c)
            def _():
                x_local(j).start()

                @pl.when(c == CHIPS - 1)
                def _():
                    xe_local(False, j).start()

            return carry

        lax.fori_loop(1, CHIPS, point, 0)

    @pl.when(c == 0)
    def _():
        first_sh.wait()

    @pl.when(odd)
    def _():
        @pl.when(c > 0)
        def _():
            shift.wait_recv()
            pass_on.start()

        own_even.wait_recv()

    @pl.when(even & (c > 0))
    def _():
        pass_on.wait_recv()

    def ahead(b, carry):
        w = pl.ds(pl.multiple_of(32 * b + 8, 8), BLOCK)
        kap = ke[w]
        ga[b] = first_part(sh[w], kap)

        @pl.when(odd)
        def _():
            g = second_part(sh[w], kap) + first_part(eb[w], kap)
            gb[b] = g[8:40, 0:COLS]

        return carry

    lax.fori_loop(0, CHIPS, ahead, 0)

    def xf_copy(lo, hi, i):
        return remote(xb.at[lo:hi], xb.at[lo:hi], xf_s.at[i], xf_r.at[i], {"tm": partner})

    spans = [(8 if i == 0 else 32 * i + 16, EXT - 8 if i == CHIPS - 1 else 32 * i + 48) for i in range(CHIPS)]
    first_x = pltpu.make_async_copy(ie.at[8 : EXT - 8], xb.at[8 : EXT - 8], own.at[1])

    @pl.when(c == 0)
    def _():
        first_x.start()
        first_x.wait()

    @pl.when(even & (c > 0))
    def _():
        for i in range(CHIPS):

            @pl.when(c == i)
            def _():
                x_local(c).wait()
                if i == CHIPS - 1:
                    xe_local(False, c).wait()

            @pl.when(c != i)
            def _():
                x_copy(i, c).wait_recv()
                if i == 0:
                    xe_copy(True, c).wait_recv()
                if i == CHIPS - 1:
                    xe_copy(False, c).wait_recv()

            xf_copy(*spans[i], i).start()

    @pl.when(odd & (c > 0))
    def _():
        for i in range(CHIPS):
            xf_copy(*spans[i], i).wait_recv()

    def finish(b, carry):
        w = pl.ds(pl.multiple_of(32 * b + 8, 8), BLOCK)
        o = pl.ds(pl.multiple_of(32 * b, 32), 32)
        kap, x = ke[w], xb[w]
        lap_x = lap(x, kap)
        mid = x + 2.0 * lap_x + ga[b]

        @pl.when(even)
        def _():
            c_out[0, o] = mid[8:40, 0:COLS]
            f_out[0, o] = (x + lap_x)[8:40, 0:COLS]

        @pl.when(odd)
        def _():
            c_out[0, o] = (x + 4.0 * lap_x)[8:40, 0:COLS] + gb[b]
            f_out[0, o] = (mid + lap(mid, kap))[8:40, 0:COLS]

        return carry

    lax.fori_loop(0, CHIPS, finish, 0)

    for cp in side + rows:
        cp.wait_send()

    @pl.when(sends_guess)
    def _():
        def sent(d, carry):
            i = lax.rem(c + d, CHIPS)
            main_copy(i, c).wait_send()
            side_copy(i, c).wait_send()
            return carry

        lax.fori_loop(1, CHIPS, sent, 0)

        @pl.when(c != 0)
        def _():
            top_copy(c).wait_send()

        @pl.when(c != CHIPS - 1)
        def _():
            bottom_copy(c).wait_send()

    @pl.when(odd)
    def _():
        @pl.when(c < CHIPS - 1)
        def _():
            shift.wait_send()

        @pl.when(c > 0)
        def _():
            pass_on.wait_send()

        def sent(m, carry):
            u_copy(m).wait_send()
            return carry

        lax.fori_loop(0, 6, sent, 0)

    @pl.when(even)
    def _():
        own_even.wait_send()

        def sent(j, carry):
            @pl.when(j != c)
            def _():
                x_copy(c, j).wait_send()

                @pl.when(c == 0)
                def _():
                    xe_copy(True, j).wait_send()

                @pl.when(c == CHIPS - 1)
                def _():
                    xe_copy(False, j).wait_send()

            return carry

        lax.fori_loop(1, CHIPS, sent, 0)

        @pl.when(c > 0)
        def _():
            for i in range(CHIPS):
                xf_copy(*spans[i], i).wait_send()


def solution(mesh):
    dma = pltpu.SemaphoreType.DMA

    def on_device(initial, kappa, guess):
        tile = jax.ShapeDtypeStruct((1, ROWS, COLS), F32)
        wide = pltpu.VMEM((EXT, WIDE), F32)
        wins = lambda n: pltpu.VMEM((n, WIN, WIDE), F32)
        return pl.pallas_call(
            kernel,
            out_shape=(tile, tile),
            in_specs=[pl.BlockSpec(memory_space=pl.ANY)] * 3,
            out_specs=(pl.BlockSpec(memory_space=pltpu.VMEM),) * 2,
            scratch_shapes=[
                wide, wide, wide,
                pltpu.VMEM((2, 96, 128), F32), pltpu.VMEM((2, 96, 128), F32),
                wins(8), wins(6), wins(7), wins(8),
                wide, wide, wide,
                pltpu.VMEM((CHIPS, BLOCK, WIDE), F32), pltpu.VMEM((CHIPS, 32, COLS), F32),
                dma((3,)), dma((2,)), dma((2,)), dma((6,)), dma((6,)),
                dma((8,)), dma((8,)), dma((8,)), dma((8,)), dma((2,)), dma((8,)), dma((2,)),
                dma, dma, dma, dma, dma, dma,
                dma((6,)), dma((6,)), dma((8,)), dma((8,)), dma((8,)), dma((2,)), dma((2,)), dma((8,)), dma((8,)),
            ],
            compiler_params=pltpu.CompilerParams(
                collective_id=0, has_side_effects=True, vmem_limit_bytes=40 * 2**20
            ),
        )(initial, kappa, guess)

    return jax.shard_map(
        on_device,
        mesh=mesh,
        in_specs=(P("sx", "sy"), P("sx", "sy"), P("tm", "sx", "sy")),
        out_specs=(P("tm", "sx", "sy"), P("tm", "sx", "sy")),
        check_vma=False,
    )
```

```python
import jax
import jax.numpy as jnp
from jax import lax
from jax.experimental import pallas as pl
from jax.experimental.pallas import tpu as pltpu
from jax.sharding import PartitionSpec as P

MESH = pl.DeviceIdType.MESH
F32 = jnp.float32
ROWS, COLS = 256, 512
MAIN, WIDE = 4, 5
EXT = ROWS + 32
CHIPS = 8
WIN = 64
BLOCK = 48
HALF = 144
EARLY = 5


def lap(v, kap, work):
    a = kap * v * v
    rows = a.shape[1]
    work[:, 8 : 8 + rows] = a
    lane = lax.broadcasted_iota(jnp.int32, a.shape, 2)
    r, l = pltpu.roll(a, 1, 2), pltpu.roll(a, 127, 2)
    before = jnp.where(lane == 0, jnp.concatenate([r[WIDE - 1 :], r[: WIDE - 1]], axis=0), r)
    after = jnp.where(lane == 127, jnp.concatenate([l[1:], l[:1]], axis=0), l)
    return (work[:, 7 : 7 + rows] + work[:, 9 : 9 + rows]) + (before + after) - 4.0 * a


def parts(p, kap, work, second):
    lap_p = lap(p, kap, work[0])
    f = p + lap_p
    v = f + lap(f, kap, work[1])
    g1 = v - p - 2.0 * lap_p
    if not second:
        return g1
    return g1, v + 2.0 * lap(v, kap, work[2]) - (p + 4.0 * lap_p)


def pack(x, back):
    x = x.reshape(4, 8, 8, 128)
    lane = lax.broadcasted_iota(jnp.int32, (4, 8, 128), 2)
    out = jnp.zeros((4, 8, 128), F32)
    for b in range(8):
        shift = (16 * b + back) % 128
        part = pltpu.roll(x[:, b], shift, 2) if shift else x[:, b]
        out = jnp.where((lane >= 16 * b) & (lane < 16 * b + 16), part, out)
    return out


def halo_rows(right, left, b):
    lane = lax.broadcasted_iota(jnp.int32, (8, 128), 1)
    r = pltpu.roll(right, 128 - 16 * b, 1) if b else right
    back = (112 - 16 * b) % 128
    l = pltpu.roll(left, back, 1) if back else left
    return jnp.where(lane < 16, r, jnp.where(lane >= 112, l, 0.0))


def unpack(dst, tiles, groups, skip, scale=None):
    for group in range(groups):
        tile, b = (group + skip) // 8, (group + skip) % 8
        r, l = tiles(0, tile), tiles(1, tile)
        if scale is not None:
            r, l = r * scale[0], l * scale[1]
        dst[MAIN, 8 * group : 8 * group + 8] = halo_rows(r, l, b)


def kernel(
    init_hbm, kap_hbm, guess_hbm, c_out, f_out,
    ie, ke, ce, sp, si, pt, gs, got, us, ur, xs, xb, ph, phs, qh, qhs, ga, gb, oc, of, w0, w1, w2,
    ld, st_s, st_r, co_s, co_r, row_s, row_r, a_s, a_r, h_s, h_r, e_s, e_r, sh_s, sh_r, eb_s, eb_r,
    u_s, u_r, x_s, x_r, xe_s, xe_r, o_s, o_r,
):
    t, sx, sy = lax.axis_index("tm"), lax.axis_index("sx"), lax.axis_index("sy")
    nx, ny = lax.axis_size("sx"), lax.axis_size("sy")
    c, p = t // 2, lax.rem(t, 2)
    even, odd = p == 0, p == 1
    up, down = lax.rem(sx + nx - 1, nx), lax.rem(sx + 1, nx)
    left, right = lax.rem(sy + ny - 1, ny), lax.rem(sy + 1, ny)
    partner = t + 1 - 2 * p
    sends_guess = t <= 12
    work = (w0, w1, w2)

    loads = [
        [
            pltpu.make_async_copy(src.at[:, 128 * k : 128 * k + 128], dst.at[k, 16 : 16 + ROWS], ld.at[MAIN * n + k])
            for k in range(MAIN)
        ]
        for n, (src, dst) in enumerate(((init_hbm, ie), (kap_hbm, ke), (guess_hbm.at[0], ce)))
    ]
    for n in (2, 1, 0):
        for cp in loads[n]:
            cp.start()

    barrier = pltpu.get_barrier_semaphore()
    got[...] = jnp.zeros(got.shape, F32)

    def greet(d, carry):
        pl.semaphore_signal(barrier, inc=1, device_id={"tm": lax.rem(t + d, 2 * CHIPS)}, device_id_type=MESH)
        return carry

    lax.fori_loop(1, 2 * CHIPS, greet, 0)
    near = [{"sx": up}, {"sx": down}, {"sy": left}, {"sy": right}]
    near += [{"sx": v, "sy": h} for v in (up, down) for h in (left, right)]
    for there in near:
        pl.semaphore_signal(barrier, inc=1, device_id=there, device_id_type=MESH)
    for w in work:
        w[...] = jnp.zeros(w.shape, F32)

    def remote(src, dst, s, r, there):
        return pltpu.make_async_remote_copy(src, dst, s, r, device_id=there, device_id_type=MESH)

    def strip_copies(n, lo, hi):
        copies = []
        for side, h in enumerate((left, right)):
            k = 2 * n + side
            f = pl.ds(lo, hi - lo)
            copies.append(remote(sp.at[side, f], si.at[side, f, 1:5], st_s.at[k], st_r.at[k], {"sy": h}))
            copies.append(remote(sp.at[side, f, 3], si.at[side, f, 0], co_s.at[2 * k], co_r.at[2 * k], {"sx": down, "sy": h}))
            copies.append(remote(sp.at[side, f, 0], si.at[side, f, 5], co_s.at[2 * k + 1], co_r.at[2 * k + 1], {"sx": up, "sy": h}))
        return copies

    def row_copies(n, ref):
        a, b, m = 2 * n, 2 * n + 1, pl.ds(0, MAIN)
        return [
            remote(ref.at[m, 16:32], ref.at[m, EXT - 16 : EXT], row_s.at[a], row_r.at[a], {"sx": up}),
            remote(ref.at[m, EXT - 32 : EXT - 16], ref.at[m, 0:16], row_s.at[b], row_r.at[b], {"sx": down}),
        ]

    def main_copy(i, slot):
        start = jnp.clip(32 * i - 8, 0, ROWS - BLOCK)
        src = ce.at[:, pl.ds(pl.multiple_of(start + 16, 8), BLOCK)]
        dst = got.at[slot, :, pl.ds(pl.multiple_of(start + 16 - 32 * i, 8), BLOCK)]
        return remote(src, dst, a_s.at[i], a_r.at[slot], {"tm": 2 * i + p})

    def side_copy(i, slot):
        return remote(pt.at[i], gs.at[slot], h_s.at[i], h_r.at[slot], {"tm": 2 * i + p})

    def top_copy(slot):
        return remote(ce.at[:, 0:16], got.at[slot, :, 0:16], e_s.at[0], e_r.at[slot], {"tm": p})

    def bottom_copy(slot):
        return remote(ce.at[:, EXT - 16 : EXT], got.at[slot, :, 48:64], e_s.at[1], e_r.at[slot], {"tm": 2 * CHIPS - 2 + p})

    guess_near = strip_copies(0, 2, 3) + row_copies(2, ce)
    other_near = strip_copies(1, 0, 2) + row_copies(1, ke) + row_copies(0, ie)

    def send_main(d, carry):
        main_copy(lax.rem(c + d, CHIPS), c).start()
        return carry

    def send_side(d, carry):
        side_copy(lax.rem(c + d, CHIPS), c).start()
        return carry

    for cp in loads[2]:
        cp.wait()
    sp[0, 2] = pack(ce[0, 16 : 16 + ROWS], 0)
    sp[1, 2] = pack(ce[MAIN - 1, 16 : 16 + ROWS], 16)
    pl.semaphore_wait(barrier, 2 * CHIPS - 1 + 8)
    for cp in guess_near:
        cp.start()

    @pl.when(sends_guess)
    def _():
        lax.fori_loop(1, EARLY, send_main, 0)

    for n, ref in ((0, ie), (1, ke)):
        for cp in loads[n]:
            cp.wait()
        sp[0, n] = pack(ref[0, 16 : 16 + ROWS], 0)
        sp[1, n] = pack(ref[MAIN - 1, 16 : 16 + ROWS], 16)
    for cp in other_near:
        cp.start()

    for cp in guess_near:
        cp.wait_recv()
    lane = lax.broadcasted_iota(jnp.int32, (8, 128), 1)
    for i in range(CHIPS):
        q, late = i // 2, i % 2
        back, cut = (96, 96) if late else (32, 32)
        for side in range(2):
            a, b = si[side, 2, q + late], si[side, 2, q + late + 1]
            pt[i, side] = jnp.where(lane < cut, pltpu.roll(a, back, 1), pltpu.roll(b, back, 1))

    @pl.when(sends_guess)
    def _():
        lax.fori_loop(1, CHIPS, send_side, 0)

        @pl.when(c != 0)
        def _():
            top_copy(c).start()

        @pl.when(c != CHIPS - 1)
        def _():
            bottom_copy(c).start()

        lax.fori_loop(EARLY, CHIPS, send_main, 0)

    at = pl.multiple_of(32 * c, 32)
    got[c] = ce[:, pl.ds(at, WIN)]
    gs[c] = pt[c]

    mine = pl.multiple_of(8 + 128 * p, 8)

    def shift(h):
        to = {"tm": jnp.minimum(t + 1 + h, 2 * CHIPS - 1)}
        return [
            remote(ce.at[:, pl.ds(8 + 128 * h, HALF)], ph.at[0:MAIN], sh_s.at[2 * h], sh_r.at[0], to),
            remote(si.at[:, 2, pl.ds(2 * h, 4)], phs, sh_s.at[2 * h + 1], sh_r.at[1], to),
        ]

    @pl.when(odd & (c < CHIPS - 1))
    def _():
        for cp in shift(0) + shift(1):
            cp.start()

    own_even = [
        remote(ce.at[:, pl.ds(136, HALF)], qh.at[0:MAIN], eb_s.at[0], eb_r.at[0], {"tm": partner}),
        remote(si.at[:, 2, pl.ds(2, 4)], qhs, eb_s.at[1], eb_r.at[1], {"tm": partner}),
    ]

    @pl.when(even)
    def _():
        for cp in own_even:
            cp.start()

    for cp in other_near:
        cp.wait_recv()
    keep = (jnp.where(sy == ny - 1, 0.0, 1.0).astype(F32), jnp.where(sy == 0, 0.0, 1.0).astype(F32))
    unpack(ke, lambda side, k: si[side, 1, k], EXT // 8, 6, keep)
    unpack(ie, lambda side, k: si[side, 0, k], EXT // 8, 6)

    @pl.when(sx == 0)
    def _():
        ke[:, 0:16] = jnp.zeros((WIDE, 16, 128), F32)

    @pl.when(sx == nx - 1)
    def _():
        ke[:, EXT - 16 : EXT] = jnp.zeros((WIDE, 16, 128), F32)

    def window(m):
        @pl.when(m != c)
        def _():
            main_copy(c, m).wait_recv()
            side_copy(c, m).wait_recv()

            @pl.when(c == 0)
            def _():
                top_copy(m).wait_recv()

            @pl.when(c == CHIPS - 1)
            def _():
                bottom_copy(m).wait_recv()

        r, l = gs[m, 0], gs[m, 1]
        side = jnp.concatenate([halo_rows(r, l, b) for b in range(8)], axis=0)
        return jnp.concatenate([got[m], side[None]], axis=0)

    def u_copy(m):
        return remote(us.at[m], ur.at[m + 1], u_s.at[m], u_r.at[m], {"tm": partner})

    half = c // 4

    def x_copy(i, j):
        dst = xb.at[:, pl.ds(pl.multiple_of(8 + 32 * lax.rem(i, 4), 8), 32)]
        return remote(xs.at[j, :, 16:48], dst, x_s.at[j], x_r.at[lax.rem(i, 4)], {"tm": 2 * j + i // 4})

    beyond = ((0, 8, 0, 0), (3, 40, 1, 0), (4, 16, 0, HALF - 8), (7, 48, 1, HALF - 8))

    def xe_copy(n, j):
        _, row, core, to = beyond[n]
        return remote(xs.at[j, :, row : row + 8], xb.at[:, to : to + 8], xe_s.at[j], xe_r.at[to // 128], {"tm": 2 * j + core})

    def for_x(j, act):
        @pl.when((j != c) | (half == 1))
        def _():
            act(x_copy(c, j))

        for n, (i, _, core, _) in enumerate(beyond):

            @pl.when((c == i) & ((j != i) | (core == 1)))
            def _():
                act(xe_copy(n, j))

    @pl.when(odd)
    def _():
        def point(m, carry):
            us[m] = parts(window(m), ke[:, pl.ds(at, WIN)], work, True)[1]
            u_copy(m).start()
            return carry

        lax.fori_loop(0, 6, point, 0)

    @pl.when(even)
    def _():
        kap0 = ke[:, pl.ds(at, WIN)]
        ur[0] = parts(ie[:, pl.ds(at, WIN)], kap0, work, True)[1]
        xs[0] = ie[:, pl.ds(at, WIN)]

        def point(j, carry):
            kap = ke[:, pl.ds(at, WIN)]
            part = parts(window(j - 1), kap, work, False)

            @pl.when(j > 1)
            def _():
                u_copy(jnp.maximum(j - 2, 0)).wait_recv()

            x = xs[j - 1]
            xs[j] = x + 4.0 * lap(x, kap, w2) + (ur[j - 1] + part)
            for_x(j, lambda cp: cp.start())

            @pl.when((j == c) & (half == 0))
            def _():
                xb[:, pl.ds(pl.multiple_of(8 + 32 * lax.rem(c, 4), 8), 32)] = xs[j, :, 16:48]

            @pl.when((j == c) & (c == 4))
            def _():
                xb[:, HALF - 8 : HALF] = xs[j, :, 16:24]

            return carry

        lax.fori_loop(1, CHIPS, point, 0)

    @pl.when(c == 0)
    def _():
        ph[...] = ie[:, pl.ds(mine, HALF)]
        xb[...] = ie[:, pl.ds(mine, HALF)]

    @pl.when(even)
    def _():
        qh[0:MAIN] = ce[:, 8 : 8 + HALF]
        unpack(qh, lambda side, k: si[side, 2, k], HALF // 8, 7)

    @pl.when(odd)
    def _():
        for cp in own_even:
            cp.wait_recv()
        unpack(qh, lambda side, k: qhs[side, k], HALF // 8, 7)

    @pl.when(c > 0)
    def _():
        for cp in shift(0):
            cp.wait_recv()
        unpack(ph, lambda side, k: phs[side, k], HALF // 8, 7)

    def ahead(b, carry):
        w = pl.ds(pl.multiple_of(32 * b, 32), BLOCK)
        kap = ke[:, pl.ds(pl.multiple_of(mine + 32 * b, 8), BLOCK)]
        g1, u = parts(ph[:, w], kap, work, True)
        ga[b] = g1
        gb[b] = u + parts(qh[:, w], kap, work, False)
        return carry

    lax.fori_loop(0, 4, ahead, 0)

    @pl.when(c > 0)
    def _():
        for k in range(4):

            @pl.when(odd | (c != k))
            def _():
                x_copy(k, c).wait_recv()

        xe_copy(0, c).wait_recv()

        @pl.when(odd | (c != 4))
        def _():
            xe_copy(2, c).wait_recv()

    def out_copy(b, n):
        o = pl.ds(pl.multiple_of(128 * p + 32 * b, 32), 32)
        src, dst = ((oc, c_out), (of, f_out))[n]
        return remote(src.at[b], dst.at[0, o], o_s.at[2 * b + n], o_r.at[2 * b + n], {"tm": partner})

    def finish(b, carry):
        w = pl.ds(pl.multiple_of(32 * b, 32), BLOCK)
        o = pl.ds(pl.multiple_of(128 * p + 32 * b, 32), 32)
        kap, x = ke[:, pl.ds(pl.multiple_of(mine + 32 * b, 8), BLOCK)], xb[:, w]
        lap_x = lap(x, kap, w0)
        mid = x + 2.0 * lap_x + ga[b]
        even_f = x + lap_x
        odd_c = x + 4.0 * lap_x + gb[b]
        odd_f = mid + lap(mid, kap, w1)

        def put(to_c, to_f, c_value, f_value):
            for k in range(MAIN):
                to_c[:, 128 * k : 128 * k + 128] = c_value[k, 8:40]
                to_f[:, 128 * k : 128 * k + 128] = f_value[k, 8:40]

        @pl.when(even)
        def _():
            put(c_out.at[0, o], f_out.at[0, o], mid, even_f)
            put(oc.at[b], of.at[b], odd_c, odd_f)

        @pl.when(odd)
        def _():
            put(c_out.at[0, o], f_out.at[0, o], odd_c, odd_f)
            put(oc.at[b], of.at[b], mid, even_f)

        out_copy(b, 0).start()
        out_copy(b, 1).start()
        return carry

    lax.fori_loop(0, 4, finish, 0)

    for cp in guess_near + other_near:
        cp.wait_send()

    @pl.when(sends_guess)
    def _():
        def sent(d, carry):
            i = lax.rem(c + d, CHIPS)
            main_copy(i, c).wait_send()
            side_copy(i, c).wait_send()
            return carry

        lax.fori_loop(1, CHIPS, sent, 0)

        @pl.when(c != 0)
        def _():
            top_copy(c).wait_send()

        @pl.when(c != CHIPS - 1)
        def _():
            bottom_copy(c).wait_send()

    @pl.when(odd)
    def _():
        @pl.when(c < CHIPS - 1)
        def _():
            for cp in shift(0) + shift(1):
                cp.wait_send()

        def sent(m, carry):
            u_copy(m).wait_send()
            return carry

        lax.fori_loop(0, 6, sent, 0)

    @pl.when(even)
    def _():
        for cp in own_even:
            cp.wait_send()

        def sent(j, carry):
            for_x(j, lambda cp: cp.wait_send())
            return carry

        lax.fori_loop(1, CHIPS, sent, 0)

    def landed(b, carry):
        for n in range(2):
            out_copy(b, n).wait()
        return carry

    lax.fori_loop(0, 4, landed, 0)


def solution(mesh):
    def dma(*shape):
        return pltpu.SemaphoreType.DMA(shape) if shape else pltpu.SemaphoreType.DMA

    def vmem(*shape):
        return pltpu.VMEM(shape, F32)

    def on_device(initial, kappa, guess):
        tile = jax.ShapeDtypeStruct((1, ROWS, COLS), F32)
        return pl.pallas_call(
            kernel,
            out_shape=(tile, tile),
            in_specs=[pl.BlockSpec(memory_space=pltpu.HBM)] * 3,
            out_specs=(pl.BlockSpec(memory_space=pltpu.VMEM),) * 2,
            scratch_shapes=[
                vmem(WIDE, EXT, 128), vmem(WIDE, EXT, 128), vmem(MAIN, EXT, 128),
                vmem(2, 3, 4, 8, 128), vmem(2, 3, 6, 8, 128), vmem(CHIPS, 2, 8, 128), vmem(CHIPS, 2, 8, 128),
                vmem(CHIPS, MAIN, WIN, 128), vmem(6, WIDE, WIN, 128), vmem(7, WIDE, WIN, 128), vmem(8, WIDE, WIN, 128),
                vmem(WIDE, HALF, 128), vmem(WIDE, HALF, 128), vmem(2, 4, 8, 128), vmem(WIDE, HALF, 128), vmem(2, 4, 8, 128),
                vmem(4, WIDE, BLOCK, 128), vmem(4, WIDE, BLOCK, 128), vmem(4, 32, COLS), vmem(4, 32, COLS),
                vmem(WIDE, WIN + 16, 128), vmem(WIDE, WIN + 16, 128), vmem(WIDE, WIN + 16, 128),
                dma(12), dma(4), dma(4), dma(8), dma(8), dma(6), dma(6),
                dma(8), dma(8), dma(8), dma(8), dma(2), dma(8), dma(4), dma(2), dma(2), dma(2),
                dma(6), dma(6), dma(8), dma(4), dma(8), dma(2), dma(8), dma(8),
            ],
            compiler_params=pltpu.CompilerParams(
                collective_id=0, has_side_effects=True, vmem_limit_bytes=67043328
            ),
        )(initial, kappa, guess)

    return jax.shard_map(
        on_device,
        mesh=mesh,
        in_specs=(P("sx", "sy"), P("sx", "sy"), P("tm", "sx", "sy")),
        out_specs=(P("tm", "sx", "sy"), P("tm", "sx", "sy")),
        check_vma=False,
    )
```

```python
import jax
import jax.numpy as jnp
from jax import lax
from jax.experimental import pallas as pl
from jax.experimental.pallas import tpu as pltpu
from jax.sharding import PartitionSpec as P

MESH = pl.DeviceIdType.MESH
F32 = jnp.float32
ROWS, COLS = 256, 512
MAIN, WIDE = 4, 5
EXT = ROWS + 32
CHIPS = 8
WIN = 64
BLOCK = 48
HALF = 144


def lap(v, kap, work):
    a = kap * v * v
    rows = a.shape[1]
    work[:, 8 : 8 + rows] = a
    lane = lax.broadcasted_iota(jnp.int32, a.shape, 2)
    r, l = pltpu.roll(a, 1, 2), pltpu.roll(a, 127, 2)
    before = jnp.where(lane == 0, jnp.concatenate([r[WIDE - 1 :], r[: WIDE - 1]], axis=0), r)
    after = jnp.where(lane == 127, jnp.concatenate([l[1:], l[:1]], axis=0), l)
    return (work[:, 7 : 7 + rows] + work[:, 9 : 9 + rows]) + (before + after) - 4.0 * a


def parts(p, kap, work, second):
    lap_p = lap(p, kap, work[0])
    f = p + lap_p
    v = f + lap(f, kap, work[1])
    g1 = v - p - 2.0 * lap_p
    if not second:
        return g1
    return g1, v + 2.0 * lap(v, kap, work[2]) - (p + 4.0 * lap_p)


def pack(x, back):
    x = x.reshape(4, 8, 8, 128)
    lane = lax.broadcasted_iota(jnp.int32, (4, 8, 128), 2)
    out = jnp.zeros((4, 8, 128), F32)
    for b in range(8):
        shift = (16 * b + back) % 128
        part = pltpu.roll(x[:, b], shift, 2) if shift else x[:, b]
        out = jnp.where((lane >= 16 * b) & (lane < 16 * b + 16), part, out)
    return out


def halo_rows(right, left, b):
    lane = lax.broadcasted_iota(jnp.int32, (8, 128), 1)
    r = pltpu.roll(right, 128 - 16 * b, 1) if b else right
    back = (112 - 16 * b) % 128
    l = pltpu.roll(left, back, 1) if back else left
    return jnp.where(lane < 16, r, jnp.where(lane >= 112, l, 0.0))


def unpack(dst, tiles, groups, skip):
    for group in range(groups):
        tile, b = (group + skip) // 8, (group + skip) % 8
        r, l = tiles(0, tile), tiles(1, tile)
        dst[MAIN, 8 * group : 8 * group + 8] = halo_rows(r, l, b)


def kernel(
    init_hbm, kap_hbm, guess_hbm, c_out, f_out,
    ie, ke, ce, sp, si, pt, gs, gx, got, gp, us, ur, xs, xb, ph, phs, qh, qhs, ga, gb, oc, of, w0, w1, w2,
    ld, st_s, st_r, co_s, co_r, row_s, row_r, a_s, a_r, h_s, h_r, e_s, e_r, k_s, k_r, sh_s, sh_r, eb_s, eb_r,
    u_s, u_r, x_s, x_r, xe_s, xe_r, o_s, o_r,
):
    t, sx, sy = lax.axis_index("tm"), lax.axis_index("sx"), lax.axis_index("sy")
    nx, ny = lax.axis_size("sx"), lax.axis_size("sy")
    c, p = t // 2, lax.rem(t, 2)
    even, odd = p == 0, p == 1
    up, down, left, right = sx - 1, sx + 1, sy - 1, sy + 1
    has_up, has_down, has_left, has_right = sx > 0, sx < nx - 1, sy > 0, sy < ny - 1
    tall, broad = has_up.astype(jnp.int32) + has_down, has_left.astype(jnp.int32) + has_right
    partner = t + 1 - 2 * p
    sends_guess = t <= 12
    work = (w0, w1, w2)

    loads = [
        [
            pltpu.make_async_copy(src.at[:, 128 * k : 128 * k + 128], dst.at[k, 16 : 16 + ROWS], ld.at[MAIN * n + k])
            for k in range(MAIN)
        ]
        for n, (src, dst) in enumerate(((init_hbm, ie), (kap_hbm, ke), (guess_hbm.at[0], ce)))
    ]
    for n in (2, 1, 0):
        for cp in loads[n]:
            cp.start()

    barrier = pltpu.get_barrier_semaphore()
    for ref in (got, si, gs, gx):
        ref[...] = jnp.zeros(ref.shape, F32)
    for ref in (ie, ke, ce):
        for rows in (slice(0, 16), slice(EXT - 16, EXT)):
            ref[:, rows] = jnp.zeros((ref.shape[0], 16, 128), F32)

    def greet(d, carry):
        pl.semaphore_signal(barrier, inc=1, device_id={"tm": lax.rem(t + d, 2 * CHIPS)}, device_id_type=MESH)
        return carry

    lax.fori_loop(1, 2 * CHIPS, greet, 0)
    for v, has_v in ((0, True), (up, has_up), (down, has_down)):
        for h, has_h in ((0, True), (left, has_left), (right, has_right)):
            there = ({"sx": v} if has_v is not True else {}) | ({"sy": h} if has_h is not True else {})
            if there:

                @pl.when(has_v & has_h)
                def _():
                    pl.semaphore_signal(barrier, inc=1, device_id=there, device_id_type=MESH)


    def greet_all(has, **there):
        @pl.when(has)
        def _():
            def signal(i, carry):
                pl.semaphore_signal(barrier, inc=1, device_id={"tm": 2 * i + p, **there}, device_id_type=MESH)
                return carry

            lax.fori_loop(0, CHIPS, signal, 0)

    for h, has_h in ((left, has_left), (right, has_right)):
        greet_all(has_h, sy=h)
    for owner, v, has_v in ((0, up, has_up), (CHIPS - 1, down, has_down)):
        greet_all((c == owner) & has_v, sx=v)
        for h, has_h in ((left, has_left), (right, has_right)):
            greet_all((c == owner) & has_v & has_h, sx=v, sy=h)
    for w in work:
        w[...] = jnp.zeros(w.shape, F32)

    def remote(src, dst, s, r, there):
        return pltpu.make_async_remote_copy(src, dst, s, r, device_id=there, device_id_type=MESH)

    def strip_copies(n, lo, hi):
        copies = []
        for side, (h, sends, gets) in enumerate(((left, has_left, has_right), (right, has_right, has_left))):
            k = 2 * n + side
            f = pl.ds(lo, hi - lo)
            cp = remote(sp.at[side, f], si.at[side, f, 1:5], st_s.at[k], st_r.at[k], {"sy": h})
            copies.append((cp, sends, gets))
            cp = remote(sp.at[side, f, 3], si.at[side, f, 0], co_s.at[2 * k], co_r.at[2 * k], {"sx": down, "sy": h})
            copies.append((cp, sends & has_down, gets & has_up))
            cp = remote(sp.at[side, f, 0], si.at[side, f, 5], co_s.at[2 * k + 1], co_r.at[2 * k + 1], {"sx": up, "sy": h})
            copies.append((cp, sends & has_up, gets & has_down))
        return copies

    def row_copies(n, ref):
        a, b, m = 2 * n, 2 * n + 1, pl.ds(0, MAIN)
        above = remote(ref.at[m, 16:32], ref.at[m, EXT - 16 : EXT], row_s.at[a], row_r.at[a], {"sx": up})
        below = remote(ref.at[m, EXT - 32 : EXT - 16], ref.at[m, 0:16], row_s.at[b], row_r.at[b], {"sx": down})
        return [(above, has_up, has_down), (below, has_down, has_up)]

    def start_near(copies):
        for cp, sends, _ in copies:
            pl.when(sends)(cp.start)

    def await_near(copies):
        for cp, _, gets in copies:
            pl.when(gets)(cp.wait_recv)

    def main_copy(i, slot):
        start = jnp.clip(32 * i - 8, 0, ROWS - BLOCK)
        src = ce.at[:, pl.ds(pl.multiple_of(start + 16, 8), BLOCK)]
        dst = got.at[slot, :, pl.ds(pl.multiple_of(start + 16 - 32 * i, 8), BLOCK)]
        return remote(src, dst, a_s.at[i], a_r.at[slot], {"tm": 2 * i + p})

    def side_copy(side, i, slot):
        there = {"tm": 2 * i + p, "sy": (left, right)[side]}
        return remote(pt.at[side, i], gs.at[slot, side], h_s.at[side, i], h_r.at[slot, side], there)

    def edge_copy(low, slot):
        if low:
            there = {"tm": p, "sx": down}
            return remote(ce.at[:, EXT - 32 : EXT - 16], got.at[slot, :, 0:16], e_s.at[0], e_r.at[slot], there)
        there = {"tm": 2 * CHIPS - 2 + p, "sx": up}
        return remote(ce.at[:, 16:32], got.at[slot, :, 48:64], e_s.at[1], e_r.at[slot], there)

    def corner_copy(low, side, slot):
        there = {"tm": p, "sx": down} if low else {"tm": 2 * CHIPS - 2 + p, "sx": up}
        there["sy"] = (left, right)[side]
        src = pt.at[side, CHIPS if low else CHIPS + 1]
        return remote(src, gx.at[slot, side], k_s.at[2 * low + side], k_r.at[slot, side], there)

    def to_owners(act):
        for side, has in enumerate((has_left, has_right)):

            @pl.when(has)
            def _():
                def one(i, carry):
                    act(side_copy(side, i, c))
                    return carry

                lax.fori_loop(0, CHIPS, one, 0)

        for low, has in enumerate((has_up, has_down)):

            @pl.when(has)
            def _():
                act(edge_copy(low, c))

            for side, beside in enumerate((has_left, has_right)):

                @pl.when(has & beside)
                def _():
                    act(corner_copy(low, side, c))

    guess_near = strip_copies(0, 2, 3) + row_copies(2, ce)
    other_near = strip_copies(1, 0, 2) + row_copies(1, ke) + row_copies(0, ie)

    def send_main(d, carry):
        main_copy(lax.rem(c + d, CHIPS), c).start()
        return carry

    for cp in loads[2]:
        cp.wait()
    sp[0, 2] = pack(ce[0, 16 : 16 + ROWS], 0)
    sp[1, 2] = pack(ce[MAIN - 1, 16 : 16 + ROWS], 16)
    lane = lax.broadcasted_iota(jnp.int32, (8, 128), 1)
    none = jnp.zeros((8, 128), F32)
    for side in range(2):
        tiles = [none] + [sp[side, 2, k] for k in range(4)] + [none]
        for i in range(CHIPS):
            q, late = i // 2, i % 2
            back, cut = (96, 96) if late else (32, 32)
            a, b = pltpu.roll(tiles[q + late], back, 1), pltpu.roll(tiles[q + late + 1], back, 1)
            pt[side, i] = jnp.where(lane < cut, a, b)
        pt[side, CHIPS] = pltpu.roll(tiles[4], 32, 1)
        pt[side, CHIPS + 1] = pltpu.roll(tiles[1], 96, 1)
    for n, ref in ((0, ie), (1, ke)):
        for cp in loads[n]:
            cp.wait()
        sp[0, n] = pack(ref[0, 16 : 16 + ROWS], 0)
        sp[1, n] = pack(ref[MAIN - 1, 16 : 16 + ROWS], 16)
    pl.semaphore_wait(barrier, 2 * CHIPS - 1 + tall + broad + tall * broad + CHIPS * broad + tall + tall * broad)

    start_near(other_near + guess_near)

    @pl.when(sends_guess)
    def _():
        to_owners(lambda cp: cp.start())
        lax.fori_loop(1, CHIPS, send_main, 0)


    at = pl.multiple_of(32 * c, 32)
    start = jnp.clip(32 * c - 8, 0, ROWS - BLOCK)
    into = pl.ds(pl.multiple_of(start + 16 - 32 * c, 8), BLOCK)
    got[c, :, into] = ce[:, pl.ds(pl.multiple_of(start + 16, 8), BLOCK)]

    await_near(guess_near)

    mine = pl.multiple_of(8 + 128 * p, 8)

    def shift(h):
        to = {"tm": jnp.minimum(t + 1 + h, 2 * CHIPS - 1)}
        return [
            remote(ce.at[:, pl.ds(8 + 128 * h, HALF)], ph.at[0:MAIN], sh_s.at[2 * h], sh_r.at[0], to),
            remote(si.at[:, 2, pl.ds(2 * h, 4)], phs, sh_s.at[2 * h + 1], sh_r.at[1], to),
        ]

    @pl.when(odd & (c < CHIPS - 1))
    def _():
        for cp in shift(0) + shift(1):
            cp.start()

    own_even = [
        remote(ce.at[:, pl.ds(136, HALF)], qh.at[0:MAIN], eb_s.at[0], eb_r.at[0], {"tm": partner}),
        remote(si.at[:, 2, pl.ds(2, 4)], qhs, eb_s.at[1], eb_r.at[1], {"tm": partner}),
    ]

    @pl.when(even)
    def _():
        for cp in own_even:
            cp.start()

    await_near(other_near)
    unpack(ke, lambda side, k: si[side, 1, k], EXT // 8, 6)
    unpack(ie, lambda side, k: si[side, 0, k], EXT // 8, 6)

    def window(m):
        @pl.when(m != c)
        def _():
            main_copy(c, m).wait_recv()

        pl.when(has_right)(lambda: side_copy(0, c, m).wait_recv())
        pl.when(has_left)(lambda: side_copy(1, c, m).wait_recv())
        outside = ((c == 0) & has_up) | ((c == CHIPS - 1) & has_down)

        @pl.when(outside)
        def _():
            edge_copy(1, m).wait_recv()

        @pl.when(outside & has_right)
        def _():
            corner_copy(1, 0, m).wait_recv()

        @pl.when(outside & has_left)
        def _():
            corner_copy(1, 1, m).wait_recv()

        outer = ((c == 0) & (lane < 32)) | ((c == CHIPS - 1) & (lane >= 96))
        r, l = (jnp.where(outer, gx[m, n], gs[m, n]) for n in range(2))
        side = jnp.concatenate([halo_rows(r, l, b) for b in range(8)], axis=0)
        return jnp.concatenate([got[m], side[None]], axis=0)

    def arrivals(count, act):
        def one(d, carry):
            m = lax.rem(c + CHIPS - d, CHIPS)

            @pl.when(m < count)
            def _():
                act(m)

            return carry

        lax.fori_loop(0, CHIPS, one, 0)

    def u_copy(m):
        return remote(us.at[m], ur.at[m + 1], u_s.at[m], u_r.at[m], {"tm": partner})

    half = c // 4

    def x_copy(i, j):
        dst = xb.at[:, pl.ds(pl.multiple_of(8 + 32 * lax.rem(i, 4), 8), 32)]
        return remote(xs.at[j, :, 16:48], dst, x_s.at[j], x_r.at[lax.rem(i, 4)], {"tm": 2 * j + i // 4})

    beyond = ((0, 8, 0, 0), (3, 40, 1, 0), (4, 16, 0, HALF - 8), (7, 48, 1, HALF - 8))

    def xe_copy(n, j):
        _, row, core, to = beyond[n]
        return remote(xs.at[j, :, row : row + 8], xb.at[:, to : to + 8], xe_s.at[j], xe_r.at[to // 128], {"tm": 2 * j + core})

    def for_x(j, act):
        @pl.when((j != c) | (half == 1))
        def _():
            act(x_copy(c, j))

        for n, (i, _, core, _) in enumerate(beyond):

            @pl.when((c == i) & ((j != i) | (core == 1)))
            def _():
                act(xe_copy(n, j))

    @pl.when(odd)
    def _():
        def point(m):
            us[m] = parts(window(m), ke[:, pl.ds(at, WIN)], work, True)[1]
            u_copy(m).start()

        arrivals(6, point)

    @pl.when(even)
    def _():
        kap0 = ke[:, pl.ds(at, WIN)]
        ur[0] = parts(ie[:, pl.ds(at, WIN)], kap0, work, True)[1]
        xs[0] = ie[:, pl.ds(at, WIN)]

        def ready(m):
            gp[m] = parts(window(m), ke[:, pl.ds(at, WIN)], work, False)

        arrivals(7, ready)

        def point(j, carry):
            @pl.when(j > 1)
            def _():
                u_copy(jnp.maximum(j - 2, 0)).wait_recv()

            x = xs[j - 1]
            xs[j] = x + 4.0 * lap(x, ke[:, pl.ds(at, WIN)], w2) + (ur[j - 1] + gp[j - 1])
            for_x(j, lambda cp: cp.start())

            @pl.when((j == c) & (half == 0))
            def _():
                xb[:, pl.ds(pl.multiple_of(8 + 32 * lax.rem(c, 4), 8), 32)] = xs[j, :, 16:48]

            @pl.when((j == c) & (c == 4))
            def _():
                xb[:, HALF - 8 : HALF] = xs[j, :, 16:24]

            return carry

        lax.fori_loop(1, CHIPS, point, 0)

    @pl.when(c == 0)
    def _():
        ph[...] = ie[:, pl.ds(mine, HALF)]
        xb[...] = ie[:, pl.ds(mine, HALF)]

    @pl.when(even)
    def _():
        qh[0:MAIN] = ce[:, 8 : 8 + HALF]
        unpack(qh, lambda side, k: si[side, 2, k], HALF // 8, 7)

    @pl.when(odd)
    def _():
        for cp in own_even:
            cp.wait_recv()
        unpack(qh, lambda side, k: qhs[side, k], HALF // 8, 7)

    @pl.when(c > 0)
    def _():
        for cp in shift(0):
            cp.wait_recv()
        unpack(ph, lambda side, k: phs[side, k], HALF // 8, 7)

    def ahead(b, carry):
        w = pl.ds(pl.multiple_of(32 * b, 32), BLOCK)
        kap = ke[:, pl.ds(pl.multiple_of(mine + 32 * b, 8), BLOCK)]
        g1, u = parts(ph[:, w], kap, work, True)
        ga[b] = g1
        gb[b] = u + parts(qh[:, w], kap, work, False)
        return carry

    lax.fori_loop(0, 4, ahead, 0)

    @pl.when(c > 0)
    def _():
        for k in range(4):

            @pl.when(odd | (c != k))
            def _():
                x_copy(k, c).wait_recv()

        xe_copy(0, c).wait_recv()

        @pl.when(odd | (c != 4))
        def _():
            xe_copy(2, c).wait_recv()

    def out_copy(b, n):
        o = pl.ds(pl.multiple_of(128 * p + 32 * b, 32), 32)
        src, dst = ((oc, c_out), (of, f_out))[n]
        return remote(src.at[b], dst.at[0, o], o_s.at[2 * b + n], o_r.at[2 * b + n], {"tm": partner})

    def finish(b, carry):
        w = pl.ds(pl.multiple_of(32 * b, 32), BLOCK)
        o = pl.ds(pl.multiple_of(128 * p + 32 * b, 32), 32)
        kap, x = ke[:, pl.ds(pl.multiple_of(mine + 32 * b, 8), BLOCK)], xb[:, w]
        lap_x = lap(x, kap, w0)
        mid = x + 2.0 * lap_x + ga[b]
        even_f = x + lap_x
        odd_c = x + 4.0 * lap_x + gb[b]
        odd_f = mid + lap(mid, kap, w1)

        def put(to_c, to_f, c_value, f_value):
            for k in range(MAIN):
                to_c[:, 128 * k : 128 * k + 128] = c_value[k, 8:40]
                to_f[:, 128 * k : 128 * k + 128] = f_value[k, 8:40]

        @pl.when(even)
        def _():
            put(c_out.at[0, o], f_out.at[0, o], mid, even_f)
            put(oc.at[b], of.at[b], odd_c, odd_f)

        @pl.when(odd)
        def _():
            put(c_out.at[0, o], f_out.at[0, o], odd_c, odd_f)
            put(oc.at[b], of.at[b], mid, even_f)

        out_copy(b, 0).start()
        out_copy(b, 1).start()
        return carry

    lax.fori_loop(0, 4, finish, 0)

    for cp, sends, _ in guess_near + other_near:
        pl.when(sends)(cp.wait_send)

    @pl.when(sends_guess)
    def _():
        def sent(d, carry):
            main_copy(lax.rem(c + d, CHIPS), c).wait_send()
            return carry

        lax.fori_loop(1, CHIPS, sent, 0)
        to_owners(lambda cp: cp.wait_send())

    @pl.when(odd)
    def _():
        @pl.when(c < CHIPS - 1)
        def _():
            for cp in shift(0) + shift(1):
                cp.wait_send()

        def sent(m, carry):
            u_copy(m).wait_send()
            return carry

        lax.fori_loop(0, 6, sent, 0)

    @pl.when(even)
    def _():
        for cp in own_even:
            cp.wait_send()

        def sent(j, carry):
            for_x(j, lambda cp: cp.wait_send())
            return carry

        lax.fori_loop(1, CHIPS, sent, 0)

    def landed(b, carry):
        for n in range(2):
            out_copy(b, n).wait()
        return carry

    lax.fori_loop(0, 4, landed, 0)


def solution(mesh):
    def dma(*shape):
        return pltpu.SemaphoreType.DMA(shape) if shape else pltpu.SemaphoreType.DMA

    def vmem(*shape):
        return pltpu.VMEM(shape, F32)

    def on_device(initial, kappa, guess):
        tile = jax.ShapeDtypeStruct((1, ROWS, COLS), F32)
        return pl.pallas_call(
            kernel,
            out_shape=(tile, tile),
            in_specs=[pl.BlockSpec(memory_space=pltpu.HBM)] * 3,
            out_specs=(pl.BlockSpec(memory_space=pltpu.VMEM),) * 2,
            scratch_shapes=[
                vmem(WIDE, EXT, 128), vmem(WIDE, EXT, 128), vmem(MAIN, EXT, 128),
                vmem(2, 3, 4, 8, 128), vmem(2, 3, 6, 8, 128), vmem(2, CHIPS + 2, 8, 128),
                vmem(CHIPS, 2, 8, 128), vmem(CHIPS, 2, 8, 128),
                vmem(CHIPS, MAIN, WIN, 128), vmem(7, WIDE, WIN, 128), vmem(6, WIDE, WIN, 128), vmem(7, WIDE, WIN, 128), vmem(8, WIDE, WIN, 128),
                vmem(WIDE, HALF, 128), vmem(WIDE, HALF, 128), vmem(2, 4, 8, 128), vmem(WIDE, HALF, 128), vmem(2, 4, 8, 128),
                vmem(4, WIDE, BLOCK, 128), vmem(4, WIDE, BLOCK, 128), vmem(4, 32, COLS), vmem(4, 32, COLS),
                vmem(WIDE, WIN + 16, 128), vmem(WIDE, WIN + 16, 128), vmem(WIDE, WIN + 16, 128),
                dma(12), dma(4), dma(4), dma(8), dma(8), dma(6), dma(6),
                dma(8), dma(8), dma(2, 8), dma(8, 2), dma(2), dma(8), dma(4), dma(8, 2), dma(4), dma(2), dma(2), dma(2),
                dma(6), dma(6), dma(8), dma(4), dma(8), dma(2), dma(8), dma(8),
            ],
            compiler_params=pltpu.CompilerParams(
                collective_id=0, has_side_effects=True, vmem_limit_bytes=67043328
            ),
        )(initial, kappa, guess)

    return jax.shard_map(
        on_device,
        mesh=mesh,
        in_specs=(P("sx", "sy"), P("sx", "sy"), P("tm", "sx", "sy")),
        out_specs=(P("tm", "sx", "sy"), P("tm", "sx", "sy")),
        check_vma=False,
    )
```

```python
import jax
import jax.numpy as jnp
from jax import lax
from jax.experimental import pallas as pl
from jax.experimental.pallas import tpu as pltpu
from jax.sharding import PartitionSpec as P

MESH = pl.DeviceIdType.MESH
F32 = jnp.float32
ROWS, COLS = 256, 512
MAIN, WIDE = 4, 5
EXT = ROWS + 32
CHIPS = 8
WIN = 64
BLOCK = 48
HALF = 144


def lap(v, kap, work):
    a = kap * v * v
    rows = a.shape[1]
    work[:, 8 : 8 + rows] = a
    lane = lax.broadcasted_iota(jnp.int32, a.shape, 2)
    r, l = pltpu.roll(a, 1, 2), pltpu.roll(a, 127, 2)
    before = jnp.where(lane == 0, jnp.concatenate([r[WIDE - 1 :], r[: WIDE - 1]], axis=0), r)
    after = jnp.where(lane == 127, jnp.concatenate([l[1:], l[:1]], axis=0), l)
    return (work[:, 7 : 7 + rows] + work[:, 9 : 9 + rows]) + (before + after) - 4.0 * a


def parts(p, kap, work, second):
    lap_p = lap(p, kap, work[0])
    f = p + lap_p
    v = f + lap(f, kap, work[1])
    g1 = v - p - 2.0 * lap_p
    if not second:
        return g1
    return g1, v + 2.0 * lap(v, kap, work[2]) - (p + 4.0 * lap_p)


def pack(x, back):
    x = x.reshape(4, 8, 8, 128)
    lane = lax.broadcasted_iota(jnp.int32, (4, 8, 128), 2)
    out = jnp.zeros((4, 8, 128), F32)
    for b in range(8):
        shift = (16 * b + back) % 128
        part = pltpu.roll(x[:, b], shift, 2) if shift else x[:, b]
        out = jnp.where((lane >= 16 * b) & (lane < 16 * b + 16), part, out)
    return out


def halo_rows(right, left, b):
    lane = lax.broadcasted_iota(jnp.int32, (8, 128), 1)
    r = pltpu.roll(right, 128 - 16 * b, 1) if b else right
    back = (112 - 16 * b) % 128
    l = pltpu.roll(left, back, 1) if back else left
    return jnp.where(lane < 16, r, jnp.where(lane >= 112, l, 0.0))


def unpack(dst, tiles, groups, skip):
    for group in range(groups):
        tile, b = (group + skip) // 8, (group + skip) % 8
        r, l = tiles(0, tile), tiles(1, tile)
        dst[MAIN, 8 * group : 8 * group + 8] = halo_rows(r, l, b)


def kernel(
    init_hbm, kap_hbm, guess_hbm, c_out, f_out,
    ie, ke, ce, sp, si, pt, gs, gx, got, gp, us, ur, xs, xb, ph, phs, qh, qhs, ga, gb, oc, of, w0, w1, w2,
    ld, st_s, st_r, co_s, co_r, row_s, row_r, a_s, a_r, h_s, h_r, e_s, e_r, k_s, k_r, sh_s, sh_r, eb_s, eb_r,
    u_s, u_r, x_s, x_r, xe_s, xe_r, o_s, o_r,
):
    t, sx, sy = lax.axis_index("tm"), lax.axis_index("sx"), lax.axis_index("sy")
    nx, ny = lax.axis_size("sx"), lax.axis_size("sy")
    c, p = t // 2, lax.rem(t, 2)
    even, odd = p == 0, p == 1
    up, down, left, right = sx - 1, sx + 1, sy - 1, sy + 1
    has_up, has_down, has_left, has_right = sx > 0, sx < nx - 1, sy > 0, sy < ny - 1
    tall, broad = has_up.astype(jnp.int32) + has_down, has_left.astype(jnp.int32) + has_right
    partner = t + 1 - 2 * p
    sends_guess = t <= 12
    work = (w0, w1, w2)

    loads = [
        [
            pltpu.make_async_copy(src.at[:, 128 * k : 128 * k + 128], dst.at[k, 16 : 16 + ROWS], ld.at[MAIN * n + k])
            for k in range(MAIN)
        ]
        for n, (src, dst) in enumerate(((init_hbm, ie), (kap_hbm, ke), (guess_hbm.at[0], ce)))
    ]
    for n in (2, 1, 0):
        for cp in loads[n]:
            cp.start()

    barrier = pltpu.get_barrier_semaphore()
    for ref in (got, si, gs, gx):
        ref[...] = jnp.zeros(ref.shape, F32)
    for ref in (ie, ke, ce):
        for rows in (slice(0, 16), slice(EXT - 16, EXT)):
            ref[:, rows] = jnp.zeros((ref.shape[0], 16, 128), F32)

    def greet(d, carry):
        pl.semaphore_signal(barrier, inc=1, device_id={"tm": lax.rem(t + d, 2 * CHIPS)}, device_id_type=MESH)
        return carry

    lax.fori_loop(1, 2 * CHIPS, greet, 0)
    for v, has_v in ((0, True), (up, has_up), (down, has_down)):
        for h, has_h in ((0, True), (left, has_left), (right, has_right)):
            there = ({"sx": v} if has_v is not True else {}) | ({"sy": h} if has_h is not True else {})
            if there:

                @pl.when(has_v & has_h)
                def _():
                    pl.semaphore_signal(barrier, inc=1, device_id=there, device_id_type=MESH)


    def greet_all(has, **there):
        @pl.when(has)
        def _():
            def signal(i, carry):
                pl.semaphore_signal(barrier, inc=1, device_id={"tm": 2 * i + p, **there}, device_id_type=MESH)
                return carry

            lax.fori_loop(0, CHIPS, signal, 0)

    for h, has_h in ((left, has_left), (right, has_right)):
        greet_all(has_h, sy=h)
    for owner, v, has_v in ((0, up, has_up), (CHIPS - 1, down, has_down)):
        greet_all((c == owner) & has_v, sx=v)
        for h, has_h in ((left, has_left), (right, has_right)):
            greet_all((c == owner) & has_v & has_h, sx=v, sy=h)
    for w in work:
        w[...] = jnp.zeros(w.shape, F32)

    def remote(src, dst, s, r, there):
        return pltpu.make_async_remote_copy(src, dst, s, r, device_id=there, device_id_type=MESH)

    def strip_copies(n, lo, hi):
        copies = []
        for side, (h, sends, gets) in enumerate(((left, has_left, has_right), (right, has_right, has_left))):
            k = 2 * n + side
            f = pl.ds(lo, hi - lo)
            cp = remote(sp.at[side, f], si.at[side, f, 1:5], st_s.at[k], st_r.at[k], {"sy": h})
            copies.append((cp, sends, gets))
            cp = remote(sp.at[side, f, 3], si.at[side, f, 0], co_s.at[2 * k], co_r.at[2 * k], {"sx": down, "sy": h})
            copies.append((cp, sends & has_down, gets & has_up))
            cp = remote(sp.at[side, f, 0], si.at[side, f, 5], co_s.at[2 * k + 1], co_r.at[2 * k + 1], {"sx": up, "sy": h})
            copies.append((cp, sends & has_up, gets & has_down))
        return copies

    def row_copies(n, ref):
        a, b, m = 2 * n, 2 * n + 1, pl.ds(0, MAIN)
        above = remote(ref.at[m, 16:32], ref.at[m, EXT - 16 : EXT], row_s.at[a], row_r.at[a], {"sx": up})
        below = remote(ref.at[m, EXT - 32 : EXT - 16], ref.at[m, 0:16], row_s.at[b], row_r.at[b], {"sx": down})
        return [(above, has_up, has_down), (below, has_down, has_up)]

    def start_near(copies):
        for cp, sends, _ in copies:
            pl.when(sends)(cp.start)

    def await_near(copies):
        for cp, _, gets in copies:
            pl.when(gets)(cp.wait_recv)

    def main_copy(i, slot):
        start = jnp.clip(32 * i - 8, 0, ROWS - BLOCK)
        src = ce.at[:, pl.ds(pl.multiple_of(start + 16, 8), BLOCK)]
        dst = got.at[slot, :, pl.ds(pl.multiple_of(start + 16 - 32 * i, 8), BLOCK)]
        return remote(src, dst, a_s.at[i], a_r.at[slot], {"tm": 2 * i + p})

    def side_copy(side, i, slot):
        there = {"tm": 2 * i + p, "sy": (left, right)[side]}
        return remote(pt.at[side, i], gs.at[slot, side], h_s.at[side, i], h_r.at[slot, side], there)

    def edge_copy(low, slot):
        if low:
            there = {"tm": p, "sx": down}
            return remote(ce.at[:, EXT - 32 : EXT - 16], got.at[slot, :, 0:16], e_s.at[0], e_r.at[slot], there)
        there = {"tm": 2 * CHIPS - 2 + p, "sx": up}
        return remote(ce.at[:, 16:32], got.at[slot, :, 48:64], e_s.at[1], e_r.at[slot], there)

    def corner_copy(low, side, slot):
        there = {"tm": p, "sx": down} if low else {"tm": 2 * CHIPS - 2 + p, "sx": up}
        there["sy"] = (left, right)[side]
        src = pt.at[side, CHIPS if low else CHIPS + 1]
        return remote(src, gx.at[slot, side], k_s.at[2 * low + side], k_r.at[slot, side], there)

    def to_owners(act):
        for side, has in enumerate((has_left, has_right)):

            @pl.when(has)
            def _():
                def one(i, carry):
                    act(side_copy(side, i, c))
                    return carry

                lax.fori_loop(0, CHIPS, one, 0)

        for low, has in enumerate((has_up, has_down)):

            @pl.when(has)
            def _():
                act(edge_copy(low, c))

            for side, beside in enumerate((has_left, has_right)):

                @pl.when(has & beside)
                def _():
                    act(corner_copy(low, side, c))

    guess_near = strip_copies(0, 2, 3) + row_copies(2, ce)
    other_near = strip_copies(1, 0, 2) + row_copies(1, ke) + row_copies(0, ie)

    def send_main(d, carry):
        main_copy(lax.rem(c + d, CHIPS), c).start()
        return carry

    for cp in loads[2]:
        cp.wait()
    sp[0, 2] = pack(ce[0, 16 : 16 + ROWS], 0)
    sp[1, 2] = pack(ce[MAIN - 1, 16 : 16 + ROWS], 16)
    lane = lax.broadcasted_iota(jnp.int32, (8, 128), 1)
    none = jnp.zeros((8, 128), F32)
    for side in range(2):
        tiles = [none] + [sp[side, 2, k] for k in range(4)] + [none]
        for i in range(CHIPS):
            q, late = i // 2, i % 2
            back, cut = (96, 96) if late else (32, 32)
            a, b = pltpu.roll(tiles[q + late], back, 1), pltpu.roll(tiles[q + late + 1], back, 1)
            pt[side, i] = jnp.where(lane < cut, a, b)
        pt[side, CHIPS] = pltpu.roll(tiles[4], 32, 1)
        pt[side, CHIPS + 1] = pltpu.roll(tiles[1], 96, 1)
    for n, ref in ((0, ie), (1, ke)):
        for cp in loads[n]:
            cp.wait()
        sp[0, n] = pack(ref[0, 16 : 16 + ROWS], 0)
        sp[1, n] = pack(ref[MAIN - 1, 16 : 16 + ROWS], 16)
    pl.semaphore_wait(barrier, 2 * CHIPS - 1 + tall + broad + tall * broad + CHIPS * broad + tall + tall * broad)

    start_near(other_near + guess_near)

    @pl.when(sends_guess)
    def _():
        to_owners(lambda cp: cp.start())
        lax.fori_loop(1, CHIPS, send_main, 0)


    at = pl.multiple_of(32 * c, 32)
    start = jnp.clip(32 * c - 8, 0, ROWS - BLOCK)
    into = pl.ds(pl.multiple_of(start + 16 - 32 * c, 8), BLOCK)
    got[c, :, into] = ce[:, pl.ds(pl.multiple_of(start + 16, 8), BLOCK)]

    await_near(guess_near)

    mine = pl.multiple_of(8 + 128 * p, 8)

    def shift(h):
        to = {"tm": jnp.minimum(t + 1 + h, 2 * CHIPS - 1)}
        return [
            remote(ce.at[:, pl.ds(8 + 128 * h, HALF)], ph.at[0:MAIN], sh_s.at[2 * h], sh_r.at[0], to),
            remote(si.at[:, 2, pl.ds(2 * h, 4)], phs, sh_s.at[2 * h + 1], sh_r.at[1], to),
        ]

    own_even = [
        remote(ce.at[:, pl.ds(136, HALF)], qh.at[0:MAIN], eb_s.at[0], eb_r.at[0], {"tm": partner}),
        remote(si.at[:, 2, pl.ds(2, 4)], qhs, eb_s.at[1], eb_r.at[1], {"tm": partner}),
    ]

    @pl.when(even)
    def _():
        for cp in own_even:
            cp.start()

    await_near(other_near)
    unpack(ke, lambda side, k: si[side, 1, k], EXT // 8, 6)
    unpack(ie, lambda side, k: si[side, 0, k], EXT // 8, 6)

    def window(m):
        @pl.when(m != c)
        def _():
            main_copy(c, m).wait_recv()

        pl.when(has_right)(lambda: side_copy(0, c, m).wait_recv())
        pl.when(has_left)(lambda: side_copy(1, c, m).wait_recv())
        outside = ((c == 0) & has_up) | ((c == CHIPS - 1) & has_down)

        @pl.when(outside)
        def _():
            edge_copy(1, m).wait_recv()

        @pl.when(outside & has_right)
        def _():
            corner_copy(1, 0, m).wait_recv()

        @pl.when(outside & has_left)
        def _():
            corner_copy(1, 1, m).wait_recv()

        outer = ((c == 0) & (lane < 32)) | ((c == CHIPS - 1) & (lane >= 96))
        r, l = (jnp.where(outer, gx[m, n], gs[m, n]) for n in range(2))
        side = jnp.concatenate([halo_rows(r, l, b) for b in range(8)], axis=0)
        return jnp.concatenate([got[m], side[None]], axis=0)

    def arrivals(count, act):
        def one(d, carry):
            m = lax.rem(c + CHIPS - d, CHIPS)

            @pl.when(m < count)
            def _():
                act(m)

            @pl.when(odd & (c < CHIPS - 1) & (d == 2))
            def _():
                for cp in shift(0) + shift(1):
                    cp.start()

            return carry

        lax.fori_loop(0, CHIPS, one, 0)

    def u_copy(m):
        return remote(us.at[m], ur.at[m + 1], u_s.at[m], u_r.at[m], {"tm": partner})

    half = c // 4

    def x_copy(i, j):
        dst = xb.at[:, pl.ds(pl.multiple_of(8 + 32 * lax.rem(i, 4), 8), 32)]
        return remote(xs.at[j, :, 16:48], dst, x_s.at[j], x_r.at[lax.rem(i, 4)], {"tm": 2 * j + i // 4})

    beyond = ((0, 8, 0, 0), (3, 40, 1, 0), (4, 16, 0, HALF - 8), (7, 48, 1, HALF - 8))

    def xe_copy(n, j):
        _, row, core, to = beyond[n]
        return remote(xs.at[j, :, row : row + 8], xb.at[:, to : to + 8], xe_s.at[j], xe_r.at[to // 128], {"tm": 2 * j + core})

    def for_x(j, act):
        @pl.when((j != c) | (half == 1))
        def _():
            act(x_copy(c, j))

        for n, (i, _, core, _) in enumerate(beyond):

            @pl.when((c == i) & ((j != i) | (core == 1)))
            def _():
                act(xe_copy(n, j))

    @pl.when(odd)
    def _():
        def point(m):
            us[m] = parts(window(m), ke[:, pl.ds(at, WIN)], work, True)[1]
            u_copy(m).start()

        arrivals(6, point)

    @pl.when(even)
    def _():
        kap0 = ke[:, pl.ds(at, WIN)]
        ur[0] = parts(ie[:, pl.ds(at, WIN)], kap0, work, True)[1]
        xs[0] = ie[:, pl.ds(at, WIN)]

        def ready(m):
            gp[m] = parts(window(m), ke[:, pl.ds(at, WIN)], work, False)

        arrivals(7, ready)

        def point(j, carry):
            @pl.when(j > 1)
            def _():
                u_copy(jnp.maximum(j - 2, 0)).wait_recv()

            x = xs[j - 1]
            xs[j] = x + 4.0 * lap(x, ke[:, pl.ds(at, WIN)], w2) + (ur[j - 1] + gp[j - 1])
            for_x(j, lambda cp: cp.start())

            @pl.when((j == c) & (half == 0))
            def _():
                xb[:, pl.ds(pl.multiple_of(8 + 32 * lax.rem(c, 4), 8), 32)] = xs[j, :, 16:48]

            @pl.when((j == c) & (c == 4))
            def _():
                xb[:, HALF - 8 : HALF] = xs[j, :, 16:24]

            return carry

        lax.fori_loop(1, CHIPS, point, 0)

    @pl.when(c == 0)
    def _():
        ph[...] = ie[:, pl.ds(mine, HALF)]
        xb[...] = ie[:, pl.ds(mine, HALF)]

    @pl.when(even)
    def _():
        qh[0:MAIN] = ce[:, 8 : 8 + HALF]
        unpack(qh, lambda side, k: si[side, 2, k], HALF // 8, 7)

    @pl.when(odd)
    def _():
        for cp in own_even:
            cp.wait_recv()
        unpack(qh, lambda side, k: qhs[side, k], HALF // 8, 7)

    @pl.when(c > 0)
    def _():
        for cp in shift(0):
            cp.wait_recv()
        unpack(ph, lambda side, k: phs[side, k], HALF // 8, 7)

    def ahead(b, carry):
        w = pl.ds(pl.multiple_of(32 * b, 32), BLOCK)
        kap = ke[:, pl.ds(pl.multiple_of(mine + 32 * b, 8), BLOCK)]
        g1, u = parts(ph[:, w], kap, work, True)
        ga[b] = g1
        gb[b] = u + parts(qh[:, w], kap, work, False)
        return carry

    lax.fori_loop(0, 4, ahead, 0)

    @pl.when(c > 0)
    def _():
        for k in range(4):

            @pl.when(odd | (c != k))
            def _():
                x_copy(k, c).wait_recv()

        xe_copy(0, c).wait_recv()

        @pl.when(odd | (c != 4))
        def _():
            xe_copy(2, c).wait_recv()

    def out_copy(b, n):
        o = pl.ds(pl.multiple_of(128 * p + 32 * b, 32), 32)
        src, dst = ((oc, c_out), (of, f_out))[n]
        return remote(src.at[b], dst.at[0, o], o_s.at[2 * b + n], o_r.at[2 * b + n], {"tm": partner})

    def finish(b, carry):
        w = pl.ds(pl.multiple_of(32 * b, 32), BLOCK)
        o = pl.ds(pl.multiple_of(128 * p + 32 * b, 32), 32)
        kap, x = ke[:, pl.ds(pl.multiple_of(mine + 32 * b, 8), BLOCK)], xb[:, w]
        lap_x = lap(x, kap, w0)
        mid = x + 2.0 * lap_x + ga[b]
        even_f = x + lap_x
        odd_c = x + 4.0 * lap_x + gb[b]
        odd_f = mid + lap(mid, kap, w1)

        def put(to_c, to_f, c_value, f_value):
            for k in range(MAIN):
                to_c[:, 128 * k : 128 * k + 128] = c_value[k, 8:40]
                to_f[:, 128 * k : 128 * k + 128] = f_value[k, 8:40]

        @pl.when(even)
        def _():
            put(c_out.at[0, o], f_out.at[0, o], mid, even_f)
            put(oc.at[b], of.at[b], odd_c, odd_f)

        @pl.when(odd)
        def _():
            put(c_out.at[0, o], f_out.at[0, o], odd_c, odd_f)
            put(oc.at[b], of.at[b], mid, even_f)

        out_copy(b, 0).start()
        out_copy(b, 1).start()
        return carry

    lax.fori_loop(0, 4, finish, 0)

    for cp, sends, _ in guess_near + other_near:
        pl.when(sends)(cp.wait_send)

    @pl.when(sends_guess)
    def _():
        def sent(d, carry):
            main_copy(lax.rem(c + d, CHIPS), c).wait_send()
            return carry

        lax.fori_loop(1, CHIPS, sent, 0)
        to_owners(lambda cp: cp.wait_send())

    @pl.when(odd)
    def _():
        @pl.when(c < CHIPS - 1)
        def _():
            for cp in shift(0) + shift(1):
                cp.wait_send()

        def sent(m, carry):
            u_copy(m).wait_send()
            return carry

        lax.fori_loop(0, 6, sent, 0)

    @pl.when(even)
    def _():
        for cp in own_even:
            cp.wait_send()

        def sent(j, carry):
            for_x(j, lambda cp: cp.wait_send())
            return carry

        lax.fori_loop(1, CHIPS, sent, 0)

    def landed(b, carry):
        for n in range(2):
            out_copy(b, n).wait()
        return carry

    lax.fori_loop(0, 4, landed, 0)


def store(c_ref, f_ref, c_hbm, f_hbm, sem):
    copies = [pltpu.make_async_copy(src, dst, sem.at[n]) for n, (src, dst) in enumerate(((c_ref, c_hbm), (f_ref, f_hbm)))]
    for cp in copies:
        cp.start()
    for cp in copies:
        cp.wait()


def solution(mesh):
    def dma(*shape):
        return pltpu.SemaphoreType.DMA(shape) if shape else pltpu.SemaphoreType.DMA

    def vmem(*shape):
        return pltpu.VMEM(shape, F32)

    def on_device(initial, kappa, guess):
        tile = jax.ShapeDtypeStruct((1, ROWS, COLS), F32)
        c, f = pl.pallas_call(
            kernel,
            out_shape=(tile, tile),
            in_specs=[pl.BlockSpec(memory_space=pltpu.HBM)] * 3,
            out_specs=(pl.BlockSpec(memory_space=pltpu.VMEM),) * 2,
            scratch_shapes=[
                vmem(WIDE, EXT, 128), vmem(WIDE, EXT, 128), vmem(MAIN, EXT, 128),
                vmem(2, 3, 4, 8, 128), vmem(2, 3, 6, 8, 128), vmem(2, CHIPS + 2, 8, 128),
                vmem(CHIPS, 2, 8, 128), vmem(CHIPS, 2, 8, 128),
                vmem(CHIPS, MAIN, WIN, 128), vmem(7, WIDE, WIN, 128), vmem(6, WIDE, WIN, 128), vmem(7, WIDE, WIN, 128), vmem(8, WIDE, WIN, 128),
                vmem(WIDE, HALF, 128), vmem(WIDE, HALF, 128), vmem(2, 4, 8, 128), vmem(WIDE, HALF, 128), vmem(2, 4, 8, 128),
                vmem(4, WIDE, BLOCK, 128), vmem(4, WIDE, BLOCK, 128), vmem(4, 32, COLS), vmem(4, 32, COLS),
                vmem(WIDE, WIN + 16, 128), vmem(WIDE, WIN + 16, 128), vmem(WIDE, WIN + 16, 128),
                dma(12), dma(4), dma(4), dma(8), dma(8), dma(6), dma(6),
                dma(8), dma(8), dma(2, 8), dma(8, 2), dma(2), dma(8), dma(4), dma(8, 2), dma(4), dma(2), dma(2), dma(2),
                dma(6), dma(6), dma(8), dma(4), dma(8), dma(2), dma(8), dma(8),
            ],
            compiler_params=pltpu.CompilerParams(
                collective_id=0, has_side_effects=True, vmem_limit_bytes=32 * 2**20
            ),
        )(*(pltpu.with_memory_space_constraint(x, pltpu.HBM) for x in (initial, kappa, guess)))
        return pl.pallas_call(
            store,
            out_shape=(tile, tile),
            in_specs=[pl.BlockSpec(memory_space=pltpu.VMEM)] * 2,
            out_specs=(pl.BlockSpec(memory_space=pltpu.HBM),) * 2,
            scratch_shapes=[dma(2)],
            compiler_params=pltpu.CompilerParams(vmem_limit_bytes=16 * 2**20),
        )(c, f)

    return jax.shard_map(
        on_device,
        mesh=mesh,
        in_specs=(P("sx", "sy"), P("sx", "sy"), P("tm", "sx", "sy")),
        out_specs=(P("tm", "sx", "sy"), P("tm", "sx", "sy")),
        check_vma=False,
    )
```

```python
import jax
import jax.numpy as jnp
from jax import lax
from jax.experimental import pallas as pl
from jax.experimental.pallas import tpu as pltpu
from jax.sharding import PartitionSpec as P

MESH = pl.DeviceIdType.MESH
F32 = jnp.float32
ROWS, COLS = 256, 512
MAIN, WIDE = 4, 5
EXT = ROWS + 32
CHIPS = 8
WIN = 64
BLOCK = 48
HALF = 144


def lap(v, kap, work):
    a = kap * v * v
    rows = a.shape[1]
    work[:, 8 : 8 + rows] = a
    lane = lax.broadcasted_iota(jnp.int32, a.shape, 2)
    r, l = pltpu.roll(a, 1, 2), pltpu.roll(a, 127, 2)
    before = jnp.where(lane == 0, jnp.concatenate([r[WIDE - 1 :], r[: WIDE - 1]], axis=0), r)
    after = jnp.where(lane == 127, jnp.concatenate([l[1:], l[:1]], axis=0), l)
    return (work[:, 7 : 7 + rows] + work[:, 9 : 9 + rows]) + (before + after) - 4.0 * a


def parts(p, kap, work, second):
    lap_p = lap(p, kap, work[0])
    f = p + lap_p
    v = f + lap(f, kap, work[1])
    g1 = v - p - 2.0 * lap_p
    if not second:
        return g1
    return g1, v + 2.0 * lap(v, kap, work[2]) - (p + 4.0 * lap_p)


def pack(x, back):
    x = x.reshape(4, 8, 8, 128)
    lane = lax.broadcasted_iota(jnp.int32, (4, 8, 128), 2)
    out = jnp.zeros((4, 8, 128), F32)
    for b in range(8):
        shift = (16 * b + back) % 128
        part = pltpu.roll(x[:, b], shift, 2) if shift else x[:, b]
        out = jnp.where((lane >= 16 * b) & (lane < 16 * b + 16), part, out)
    return out


def halo_rows(right, left, b):
    lane = lax.broadcasted_iota(jnp.int32, (8, 128), 1)
    r = pltpu.roll(right, 128 - 16 * b, 1) if b else right
    back = (112 - 16 * b) % 128
    l = pltpu.roll(left, back, 1) if back else left
    return jnp.where(lane < 16, r, jnp.where(lane >= 112, l, 0.0))


def unpack(dst, tiles, groups, skip):
    for group in range(groups):
        tile, b = (group + skip) // 8, (group + skip) % 8
        r, l = tiles(0, tile), tiles(1, tile)
        dst[MAIN, 8 * group : 8 * group + 8] = halo_rows(r, l, b)


def kernel(
    init_hbm, kap_hbm, guess_hbm, c_out, f_out,
    ie, ke, ce, sp, si, pt, gs, gx, got, gp, us, ur, xs, xb, ph, phs, qh, qhs, ga, gb, oc, of, w0, w1, w2,
    ld, st_s, st_r, co_s, co_r, row_s, row_r, a_s, a_r, h_s, h_r, e_s, e_r, k_s, k_r, sh_s, sh_r, eb_s, eb_r,
    u_s, u_r, x_s, x_r, xe_s, xe_r, o_s, o_r,
):
    t, sx, sy = lax.axis_index("tm"), lax.axis_index("sx"), lax.axis_index("sy")
    nx, ny = lax.axis_size("sx"), lax.axis_size("sy")
    c, p = t // 2, lax.rem(t, 2)
    even, odd = p == 0, p == 1
    up, down, left, right = sx - 1, sx + 1, sy - 1, sy + 1
    has_up, has_down, has_left, has_right = sx > 0, sx < nx - 1, sy > 0, sy < ny - 1
    tall, broad = has_up.astype(jnp.int32) + has_down, has_left.astype(jnp.int32) + has_right
    partner = t + 1 - 2 * p
    sends_guess = t <= 12
    work = (w0, w1, w2)

    loads = [
        [
            pltpu.make_async_copy(src.at[:, 128 * k : 128 * k + 128], dst.at[k, 16 : 16 + ROWS], ld.at[MAIN * n + k])
            for k in range(MAIN)
        ]
        for n, (src, dst) in enumerate(((init_hbm, ie), (kap_hbm, ke), (guess_hbm.at[0], ce)))
    ]
    for n in (2, 1, 0):
        for cp in loads[n]:
            cp.start()

    barrier = pltpu.get_barrier_semaphore()
    for ref in (got, si, gs, gx):
        ref[...] = jnp.zeros(ref.shape, F32)
    for ref in (ie, ke, ce):
        for rows in (slice(0, 16), slice(EXT - 16, EXT)):
            ref[:, rows] = jnp.zeros((ref.shape[0], 16, 128), F32)

    def greet(d, carry):
        pl.semaphore_signal(barrier, inc=1, device_id={"tm": lax.rem(t + d, 2 * CHIPS)}, device_id_type=MESH)
        return carry

    lax.fori_loop(1, 2 * CHIPS, greet, 0)
    for v, has_v in ((0, True), (up, has_up), (down, has_down)):
        for h, has_h in ((0, True), (left, has_left), (right, has_right)):
            there = ({"sx": v} if has_v is not True else {}) | ({"sy": h} if has_h is not True else {})
            if there:

                @pl.when(has_v & has_h)
                def _():
                    pl.semaphore_signal(barrier, inc=1, device_id=there, device_id_type=MESH)


    def greet_all(has, **there):
        @pl.when(has)
        def _():
            def signal(i, carry):
                pl.semaphore_signal(barrier, inc=1, device_id={"tm": 2 * i + p, **there}, device_id_type=MESH)
                return carry

            lax.fori_loop(0, CHIPS, signal, 0)

    for h, has_h in ((left, has_left), (right, has_right)):
        greet_all(has_h, sy=h)
    for owner, v, has_v in ((0, up, has_up), (CHIPS - 1, down, has_down)):
        greet_all((c == owner) & has_v, sx=v)
        for h, has_h in ((left, has_left), (right, has_right)):
            greet_all((c == owner) & has_v & has_h, sx=v, sy=h)
    for w in work:
        w[...] = jnp.zeros(w.shape, F32)

    def remote(src, dst, s, r, there):
        return pltpu.make_async_remote_copy(src, dst, s, r, device_id=there, device_id_type=MESH)

    def strip_copies(n, lo, hi):
        copies = []
        for side, (h, sends, gets) in enumerate(((left, has_left, has_right), (right, has_right, has_left))):
            k = 2 * n + side
            f = pl.ds(lo, hi - lo)
            cp = remote(sp.at[side, f], si.at[side, f, 1:5], st_s.at[k], st_r.at[k], {"sy": h})
            copies.append((cp, sends, gets))
            cp = remote(sp.at[side, f, 3], si.at[side, f, 0], co_s.at[2 * k], co_r.at[2 * k], {"sx": down, "sy": h})
            copies.append((cp, sends & has_down, gets & has_up))
            cp = remote(sp.at[side, f, 0], si.at[side, f, 5], co_s.at[2 * k + 1], co_r.at[2 * k + 1], {"sx": up, "sy": h})
            copies.append((cp, sends & has_up, gets & has_down))
        return copies

    def row_copies(n, ref, deep=16):
        a, b, m = 2 * n, 2 * n + 1, pl.ds(0, MAIN)
        above = remote(ref.at[m, 16 : 16 + deep], ref.at[m, EXT - 16 : EXT - 16 + deep], row_s.at[a], row_r.at[a], {"sx": up})
        below = remote(ref.at[m, EXT - 16 - deep : EXT - 16], ref.at[m, 16 - deep : 16], row_s.at[b], row_r.at[b], {"sx": down})
        return [(above, has_up, has_down), (below, has_down, has_up)]

    def start_near(copies):
        for cp, sends, _ in copies:
            pl.when(sends)(cp.start)

    def await_near(copies):
        for cp, _, gets in copies:
            pl.when(gets)(cp.wait_recv)

    def main_copy(i, slot):
        start = jnp.clip(32 * i - 8, 0, ROWS - BLOCK)
        src = ce.at[:, pl.ds(pl.multiple_of(start + 16, 8), BLOCK)]
        dst = got.at[slot, :, pl.ds(pl.multiple_of(start + 16 - 32 * i, 8), BLOCK)]
        return remote(src, dst, a_s.at[i], a_r.at[slot], {"tm": 2 * i + p})

    def side_copy(side, i, slot):
        there = {"tm": 2 * i + p, "sy": (left, right)[side]}
        return remote(pt.at[side, i], gs.at[slot, side], h_s.at[side, i], h_r.at[slot, side], there)

    def edge_copy(low, slot):
        if low:
            there = {"tm": p, "sx": down}
            return remote(ce.at[:, EXT - 32 : EXT - 16], got.at[slot, :, 0:16], e_s.at[0], e_r.at[slot], there)
        there = {"tm": 2 * CHIPS - 2 + p, "sx": up}
        return remote(ce.at[:, 16:32], got.at[slot, :, 48:64], e_s.at[1], e_r.at[slot], there)

    def corner_copy(low, side, slot):
        there = {"tm": p, "sx": down} if low else {"tm": 2 * CHIPS - 2 + p, "sx": up}
        there["sy"] = (left, right)[side]
        src = pt.at[side, CHIPS if low else CHIPS + 1]
        return remote(src, gx.at[slot, side], k_s.at[2 * low + side], k_r.at[slot, side], there)

    def to_owners(act):
        for side, has in enumerate((has_left, has_right)):

            @pl.when(has)
            def _():
                def one(i, carry):
                    act(side_copy(side, i, c))
                    return carry

                lax.fori_loop(0, CHIPS, one, 0)

        for low, has in enumerate((has_up, has_down)):

            @pl.when(has)
            def _():
                act(edge_copy(low, c))

            for side, beside in enumerate((has_left, has_right)):

                @pl.when(has & beside)
                def _():
                    act(corner_copy(low, side, c))

    guess_near = strip_copies(0, 2, 3) + row_copies(2, ce, 8)
    other_near = strip_copies(1, 1, 2) + row_copies(1, ke)
    uses_initial = even | (c == 0)
    for cp, sends, gets in strip_copies(2, 0, 1) + row_copies(0, ie):
        other_near.append((cp, sends & uses_initial, gets & uses_initial))

    def send_main(d, carry):
        main_copy(lax.rem(c + d, CHIPS), c).start()
        return carry

    for cp in loads[2]:
        cp.wait()
    sp[0, 2] = pack(ce[0, 16 : 16 + ROWS], 0)
    sp[1, 2] = pack(ce[MAIN - 1, 16 : 16 + ROWS], 16)
    lane = lax.broadcasted_iota(jnp.int32, (8, 128), 1)
    none = jnp.zeros((8, 128), F32)
    for side in range(2):
        tiles = [none] + [sp[side, 2, k] for k in range(4)] + [none]
        for i in range(CHIPS):
            q, late = i // 2, i % 2
            back, cut = (96, 96) if late else (32, 32)
            a, b = pltpu.roll(tiles[q + late], back, 1), pltpu.roll(tiles[q + late + 1], back, 1)
            pt[side, i] = jnp.where(lane < cut, a, b)
        pt[side, CHIPS] = pltpu.roll(tiles[4], 32, 1)
        pt[side, CHIPS + 1] = pltpu.roll(tiles[1], 96, 1)
    for n, ref in ((0, ie), (1, ke)):
        for cp in loads[n]:
            cp.wait()
        sp[0, n] = pack(ref[0, 16 : 16 + ROWS], 0)
        sp[1, n] = pack(ref[MAIN - 1, 16 : 16 + ROWS], 16)
    pl.semaphore_wait(barrier, 2 * CHIPS - 1 + tall + broad + tall * broad + CHIPS * broad + tall + tall * broad)

    start_near(other_near + guess_near)

    @pl.when(sends_guess)
    def _():
        to_owners(lambda cp: cp.start())
        lax.fori_loop(1, CHIPS, send_main, 0)


    at = pl.multiple_of(32 * c, 32)
    start = jnp.clip(32 * c - 8, 0, ROWS - BLOCK)
    into = pl.ds(pl.multiple_of(start + 16 - 32 * c, 8), BLOCK)
    got[c, :, into] = ce[:, pl.ds(pl.multiple_of(start + 16, 8), BLOCK)]

    await_near(guess_near)

    mine = pl.multiple_of(8 + 128 * p, 8)

    def shift(h):
        to = {"tm": jnp.minimum(t + 1 + h, 2 * CHIPS - 1)}
        return [
            remote(ce.at[:, pl.ds(8 + 128 * h, HALF)], ph.at[0:MAIN], sh_s.at[2 * h], sh_r.at[0], to),
            remote(si.at[:, 2, pl.ds(2 * h, 4)], phs, sh_s.at[2 * h + 1], sh_r.at[1], to),
        ]

    own_even = [
        remote(ce.at[:, pl.ds(136, HALF)], qh.at[0:MAIN], eb_s.at[0], eb_r.at[0], {"tm": partner}),
        remote(si.at[:, 2, pl.ds(2, 4)], qhs, eb_s.at[1], eb_r.at[1], {"tm": partner}),
    ]

    @pl.when(even)
    def _():
        for cp in own_even:
            cp.start()

    await_near(other_near)
    unpack(ke, lambda side, k: si[side, 1, k], EXT // 8, 6)

    @pl.when(uses_initial)
    def _():
        unpack(ie, lambda side, k: si[side, 0, k], EXT // 8, 6)

    def window(m):
        @pl.when(m != c)
        def _():
            main_copy(c, m).wait_recv()

        pl.when(has_right)(lambda: side_copy(0, c, m).wait_recv())
        pl.when(has_left)(lambda: side_copy(1, c, m).wait_recv())
        outside = ((c == 0) & has_up) | ((c == CHIPS - 1) & has_down)

        @pl.when(outside)
        def _():
            edge_copy(1, m).wait_recv()

        @pl.when(outside & has_right)
        def _():
            corner_copy(1, 0, m).wait_recv()

        @pl.when(outside & has_left)
        def _():
            corner_copy(1, 1, m).wait_recv()

        outer = ((c == 0) & (lane < 32)) | ((c == CHIPS - 1) & (lane >= 96))
        r, l = (jnp.where(outer, gx[m, n], gs[m, n]) for n in range(2))
        side = jnp.concatenate([halo_rows(r, l, b) for b in range(8)], axis=0)
        return jnp.concatenate([got[m], side[None]], axis=0)

    def arrivals(count, act):
        def one(d, carry):
            m = lax.rem(c + CHIPS - d, CHIPS)

            @pl.when(m < count)
            def _():
                act(m)

            @pl.when(odd & (c < CHIPS - 1) & (d == 2))
            def _():
                for cp in shift(0) + shift(1):
                    cp.start()

            return carry

        lax.fori_loop(0, CHIPS, one, 0)

    def u_copy(m):
        return remote(us.at[m], ur.at[m + 1], u_s.at[m], u_r.at[m], {"tm": partner})

    half = c // 4

    def x_copy(i, j):
        dst = xb.at[:, pl.ds(pl.multiple_of(8 + 32 * lax.rem(i, 4), 8), 32)]
        return remote(xs.at[j, :, 16:48], dst, x_s.at[j], x_r.at[lax.rem(i, 4)], {"tm": 2 * j + i // 4})

    beyond = ((0, 8, 0, 0), (3, 40, 1, 0), (4, 16, 0, HALF - 8), (7, 48, 1, HALF - 8))

    def xe_copy(n, j):
        _, row, core, to = beyond[n]
        return remote(xs.at[j, :, row : row + 8], xb.at[:, to : to + 8], xe_s.at[j], xe_r.at[to // 128], {"tm": 2 * j + core})

    def for_x(j, act):
        @pl.when((j != c) | (half == 1))
        def _():
            act(x_copy(c, j))

        for n, (i, _, core, _) in enumerate(beyond):

            @pl.when((c == i) & ((j != i) | (core == 1)))
            def _():
                act(xe_copy(n, j))

    @pl.when(odd)
    def _():
        def point(m):
            us[m] = parts(window(m), ke[:, pl.ds(at, WIN)], work, True)[1]
            u_copy(m).start()

        arrivals(6, point)

    @pl.when(even)
    def _():
        kap0 = ke[:, pl.ds(at, WIN)]
        ur[0] = parts(ie[:, pl.ds(at, WIN)], kap0, work, True)[1]
        xs[0] = ie[:, pl.ds(at, WIN)]

        def ready(m):
            gp[m] = parts(window(m), ke[:, pl.ds(at, WIN)], work, False)

        arrivals(7, ready)

        def point(j, carry):
            @pl.when(j > 1)
            def _():
                u_copy(jnp.maximum(j - 2, 0)).wait_recv()

            x = xs[j - 1]
            xs[j] = x + 4.0 * lap(x, ke[:, pl.ds(at, WIN)], w2) + (ur[j - 1] + gp[j - 1])
            for_x(j, lambda cp: cp.start())

            @pl.when((j == c) & (half == 0))
            def _():
                xb[:, pl.ds(pl.multiple_of(8 + 32 * lax.rem(c, 4), 8), 32)] = xs[j, :, 16:48]

            @pl.when((j == c) & (c == 4))
            def _():
                xb[:, HALF - 8 : HALF] = xs[j, :, 16:24]

            return carry

        lax.fori_loop(1, CHIPS, point, 0)

    @pl.when(c == 0)
    def _():
        ph[...] = ie[:, pl.ds(mine, HALF)]
        xb[...] = ie[:, pl.ds(mine, HALF)]

    @pl.when(even)
    def _():
        qh[0:MAIN] = ce[:, 8 : 8 + HALF]
        unpack(qh, lambda side, k: si[side, 2, k], HALF // 8, 7)

    @pl.when(odd)
    def _():
        for cp in own_even:
            cp.wait_recv()
        unpack(qh, lambda side, k: qhs[side, k], HALF // 8, 7)

    @pl.when(c > 0)
    def _():
        for cp in shift(0):
            cp.wait_recv()
        unpack(ph, lambda side, k: phs[side, k], HALF // 8, 7)

    def ahead(b, carry):
        w = pl.ds(pl.multiple_of(32 * b, 32), BLOCK)
        kap = ke[:, pl.ds(pl.multiple_of(mine + 32 * b, 8), BLOCK)]
        g1, u = parts(ph[:, w], kap, work, True)
        ga[b] = g1
        gb[b] = u + parts(qh[:, w], kap, work, False)
        return carry

    lax.fori_loop(0, 4, ahead, 0)

    @pl.when(c > 0)
    def _():
        for k in range(4):

            @pl.when(odd | (c != k))
            def _():
                x_copy(k, c).wait_recv()

        xe_copy(0, c).wait_recv()

        @pl.when(odd | (c != 4))
        def _():
            xe_copy(2, c).wait_recv()

    def out_copy(b, n):
        o = pl.ds(pl.multiple_of(128 * p + 32 * b, 32), 32)
        src, dst = ((oc, c_out), (of, f_out))[n]
        return remote(src.at[b], dst.at[0, o], o_s.at[2 * b + n], o_r.at[2 * b + n], {"tm": partner})

    def finish(b, carry):
        w = pl.ds(pl.multiple_of(32 * b, 32), BLOCK)
        o = pl.ds(pl.multiple_of(128 * p + 32 * b, 32), 32)
        kap, x = ke[:, pl.ds(pl.multiple_of(mine + 32 * b, 8), BLOCK)], xb[:, w]
        lap_x = lap(x, kap, w0)
        mid = x + 2.0 * lap_x + ga[b]
        even_f = x + lap_x
        odd_c = x + 4.0 * lap_x + gb[b]
        odd_f = mid + lap(mid, kap, w1)

        def put(to_c, to_f, c_value, f_value):
            for k in range(MAIN):
                to_c[:, 128 * k : 128 * k + 128] = c_value[k, 8:40]
                to_f[:, 128 * k : 128 * k + 128] = f_value[k, 8:40]

        @pl.when(even)
        def _():
            put(c_out.at[0, o], f_out.at[0, o], mid, even_f)
            put(oc.at[b], of.at[b], odd_c, odd_f)

        @pl.when(odd)
        def _():
            put(c_out.at[0, o], f_out.at[0, o], odd_c, odd_f)
            put(oc.at[b], of.at[b], mid, even_f)

        out_copy(b, 0).start()
        out_copy(b, 1).start()
        return carry

    lax.fori_loop(0, 4, finish, 0)

    for cp, sends, _ in guess_near + other_near:
        pl.when(sends)(cp.wait_send)

    @pl.when(sends_guess)
    def _():
        def sent(d, carry):
            main_copy(lax.rem(c + d, CHIPS), c).wait_send()
            return carry

        lax.fori_loop(1, CHIPS, sent, 0)
        to_owners(lambda cp: cp.wait_send())

    @pl.when(odd)
    def _():
        @pl.when(c < CHIPS - 1)
        def _():
            for cp in shift(0) + shift(1):
                cp.wait_send()

        def sent(m, carry):
            u_copy(m).wait_send()
            return carry

        lax.fori_loop(0, 6, sent, 0)

    @pl.when(even)
    def _():
        for cp in own_even:
            cp.wait_send()

        def sent(j, carry):
            for_x(j, lambda cp: cp.wait_send())
            return carry

        lax.fori_loop(1, CHIPS, sent, 0)

    def landed(b, carry):
        for n in range(2):
            out_copy(b, n).wait()
        return carry

    lax.fori_loop(0, 4, landed, 0)


def store(c_ref, f_ref, c_hbm, f_hbm, sem):
    copies = [pltpu.make_async_copy(src, dst, sem.at[n]) for n, (src, dst) in enumerate(((c_ref, c_hbm), (f_ref, f_hbm)))]
    for cp in copies:
        cp.start()
    for cp in copies:
        cp.wait()


def solution(mesh):
    def dma(*shape):
        return pltpu.SemaphoreType.DMA(shape) if shape else pltpu.SemaphoreType.DMA

    def vmem(*shape):
        return pltpu.VMEM(shape, F32)

    def on_device(initial, kappa, guess):
        tile = jax.ShapeDtypeStruct((1, ROWS, COLS), F32)
        c, f = pl.pallas_call(
            kernel,
            out_shape=(tile, tile),
            in_specs=[pl.BlockSpec(memory_space=pltpu.HBM)] * 3,
            out_specs=(pl.BlockSpec(memory_space=pltpu.VMEM),) * 2,
            scratch_shapes=[
                vmem(WIDE, EXT, 128), vmem(WIDE, EXT, 128), vmem(MAIN, EXT, 128),
                vmem(2, 3, 4, 8, 128), vmem(2, 3, 6, 8, 128), vmem(2, CHIPS + 2, 8, 128),
                vmem(CHIPS, 2, 8, 128), vmem(CHIPS, 2, 8, 128),
                vmem(CHIPS, MAIN, WIN, 128), vmem(7, WIDE, WIN, 128), vmem(6, WIDE, WIN, 128), vmem(7, WIDE, WIN, 128), vmem(8, WIDE, WIN, 128),
                vmem(WIDE, HALF, 128), vmem(WIDE, HALF, 128), vmem(2, 4, 8, 128), vmem(WIDE, HALF, 128), vmem(2, 4, 8, 128),
                vmem(4, WIDE, BLOCK, 128), vmem(4, WIDE, BLOCK, 128), vmem(4, 32, COLS), vmem(4, 32, COLS),
                vmem(WIDE, WIN + 16, 128), vmem(WIDE, WIN + 16, 128), vmem(WIDE, WIN + 16, 128),
                dma(12), dma(6), dma(6), dma(12), dma(12), dma(6), dma(6),
                dma(8), dma(8), dma(2, 8), dma(8, 2), dma(2), dma(8), dma(4), dma(8, 2), dma(4), dma(2), dma(2), dma(2),
                dma(6), dma(6), dma(8), dma(4), dma(8), dma(2), dma(8), dma(8),
            ],
            compiler_params=pltpu.CompilerParams(
                collective_id=0, has_side_effects=True, vmem_limit_bytes=32 * 2**20
            ),
        )(*(pltpu.with_memory_space_constraint(x, pltpu.HBM) for x in (initial, kappa, guess)))
        return pl.pallas_call(
            store,
            out_shape=(tile, tile),
            in_specs=[pl.BlockSpec(memory_space=pltpu.VMEM)] * 2,
            out_specs=(pl.BlockSpec(memory_space=pltpu.HBM),) * 2,
            scratch_shapes=[dma(2)],
            compiler_params=pltpu.CompilerParams(vmem_limit_bytes=16 * 2**20),
        )(c, f)

    return jax.shard_map(
        on_device,
        mesh=mesh,
        in_specs=(P("sx", "sy"), P("sx", "sy"), P("tm", "sx", "sy")),
        out_specs=(P("tm", "sx", "sy"), P("tm", "sx", "sy")),
        check_vma=False,
    )
```

```python
import jax
import jax.numpy as jnp
from jax import lax
from jax.experimental import pallas as pl
from jax.experimental.pallas import tpu as pltpu
from jax.sharding import PartitionSpec as P

MESH = pl.DeviceIdType.MESH
F32 = jnp.float32
ROWS, COLS = 256, 512
MAIN, WIDE = 4, 5
EXT = ROWS + 32
CHIPS = 8
WIN = 64
BLOCK = 48
HALF = 144


def lap(v, kap, work):
    a = kap * v * v
    rows = a.shape[1]
    work[:, 8 : 8 + rows] = a
    lane = lax.broadcasted_iota(jnp.int32, a.shape, 2)
    r, l = pltpu.roll(a, 1, 2), pltpu.roll(a, 127, 2)
    before = jnp.where(lane == 0, jnp.concatenate([r[WIDE - 1 :], r[: WIDE - 1]], axis=0), r)
    after = jnp.where(lane == 127, jnp.concatenate([l[1:], l[:1]], axis=0), l)
    return (work[:, 7 : 7 + rows] + work[:, 9 : 9 + rows]) + (before + after) - 4.0 * a


def parts(p, kap, work, second):
    lap_p = lap(p, kap, work[0])
    f = p + lap_p
    v = f + lap(f, kap, work[1])
    g1 = v - p - 2.0 * lap_p
    if not second:
        return g1
    return g1, v + 2.0 * lap(v, kap, work[2]) - (p + 4.0 * lap_p)


def pack(x, back):
    x = x.reshape(4, 8, 8, 128)
    lane = lax.broadcasted_iota(jnp.int32, (4, 8, 128), 2)
    out = jnp.zeros((4, 8, 128), F32)
    for b in range(8):
        shift = (16 * b + back) % 128
        part = pltpu.roll(x[:, b], shift, 2) if shift else x[:, b]
        out = jnp.where((lane >= 16 * b) & (lane < 16 * b + 16), part, out)
    return out


def halo_rows(right, left, b):
    lane = lax.broadcasted_iota(jnp.int32, (8, 128), 1)
    r = pltpu.roll(right, 128 - 16 * b, 1) if b else right
    back = (112 - 16 * b) % 128
    l = pltpu.roll(left, back, 1) if back else left
    return jnp.where(lane < 16, r, jnp.where(lane >= 112, l, 0.0))


def unpack(dst, tiles, groups, skip):
    for group in range(groups):
        tile, b = (group + skip) // 8, (group + skip) % 8
        r, l = tiles(0, tile), tiles(1, tile)
        dst[MAIN, 8 * group : 8 * group + 8] = halo_rows(r, l, b)


def kernel(
    init_hbm, kap_hbm, guess_hbm, c_out, f_out,
    ie, ke, ce, sp, si, pt, gs, gx, got, gp, us, ur, xs, xb, ph, phs, qh, qhs, ga, gb, oc, of, w0, w1, w2,
    ld, st_s, st_r, co_s, co_r, row_s, row_r, a_s, a_r, h_s, h_r, e_s, e_r, k_s, k_r, sh_s, sh_r, eb_s, eb_r,
    u_s, u_r, x_s, x_r, xe_s, xe_r, o_s, o_r,
):
    t, sx, sy = lax.axis_index("tm"), lax.axis_index("sx"), lax.axis_index("sy")
    nx, ny = lax.axis_size("sx"), lax.axis_size("sy")
    c, p = t // 2, lax.rem(t, 2)
    even, odd = p == 0, p == 1
    up, down, left, right = sx - 1, sx + 1, sy - 1, sy + 1
    has_up, has_down, has_left, has_right = sx > 0, sx < nx - 1, sy > 0, sy < ny - 1
    tall, broad = has_up.astype(jnp.int32) + has_down, has_left.astype(jnp.int32) + has_right
    partner = t + 1 - 2 * p
    sends_guess = t <= 12
    work = (w0, w1, w2)

    loads = [
        [
            pltpu.make_async_copy(src.at[:, 128 * k : 128 * k + 128], dst.at[k, 16 : 16 + ROWS], ld.at[MAIN * n + k])
            for k in range(MAIN)
        ]
        for n, (src, dst) in enumerate(((init_hbm, ie), (kap_hbm, ke), (guess_hbm.at[0], ce)))
    ]
    for n in (2, 1, 0):
        for cp in loads[n]:
            cp.start()

    barrier = pltpu.get_barrier_semaphore()
    for ref in (si, gs, gx):
        ref[...] = jnp.zeros(ref.shape, F32)
    for rows in (slice(0, 16), slice(WIN - 16, WIN)):
        got[:, :, rows] = jnp.zeros((CHIPS, MAIN, 16, 128), F32)
    for ref in (ie, ke, ce):
        for rows in (slice(0, 16), slice(EXT - 16, EXT)):
            ref[:, rows] = jnp.zeros((ref.shape[0], 16, 128), F32)

    def greet(d, carry):
        pl.semaphore_signal(barrier, inc=1, device_id={"tm": lax.rem(t + d, 2 * CHIPS)}, device_id_type=MESH)
        return carry

    lax.fori_loop(1, 2 * CHIPS, greet, 0)
    for v, has_v in ((0, True), (up, has_up), (down, has_down)):
        for h, has_h in ((0, True), (left, has_left), (right, has_right)):
            there = ({"sx": v} if has_v is not True else {}) | ({"sy": h} if has_h is not True else {})
            if there:

                @pl.when(has_v & has_h)
                def _():
                    pl.semaphore_signal(barrier, inc=1, device_id=there, device_id_type=MESH)


    def greet_all(has, **there):
        @pl.when(has)
        def _():
            def signal(i, carry):
                pl.semaphore_signal(barrier, inc=1, device_id={"tm": 2 * i + p, **there}, device_id_type=MESH)
                return carry

            lax.fori_loop(0, CHIPS, signal, 0)

    for h, has_h in ((left, has_left), (right, has_right)):
        greet_all(has_h, sy=h)
    for owner, v, has_v in ((0, up, has_up), (CHIPS - 1, down, has_down)):
        greet_all((c == owner) & has_v, sx=v)
        for h, has_h in ((left, has_left), (right, has_right)):
            greet_all((c == owner) & has_v & has_h, sx=v, sy=h)
    for w in work:
        w[...] = jnp.zeros(w.shape, F32)

    def remote(src, dst, s, r, there):
        return pltpu.make_async_remote_copy(src, dst, s, r, device_id=there, device_id_type=MESH)

    def strip_copies(n, lo, hi):
        copies = []
        for side, (h, sends, gets) in enumerate(((left, has_left, has_right), (right, has_right, has_left))):
            k = 2 * n + side
            f = pl.ds(lo, hi - lo)
            cp = remote(sp.at[side, f], si.at[side, f, 1:5], st_s.at[k], st_r.at[k], {"sy": h})
            copies.append((cp, sends, gets))
            cp = remote(sp.at[side, f, 3], si.at[side, f, 0], co_s.at[2 * k], co_r.at[2 * k], {"sx": down, "sy": h})
            copies.append((cp, sends & has_down, gets & has_up))
            cp = remote(sp.at[side, f, 0], si.at[side, f, 5], co_s.at[2 * k + 1], co_r.at[2 * k + 1], {"sx": up, "sy": h})
            copies.append((cp, sends & has_up, gets & has_down))
        return copies

    def row_copies(n, ref, deep=16):
        a, b, m = 2 * n, 2 * n + 1, pl.ds(0, MAIN)
        above = remote(ref.at[m, 16 : 16 + deep], ref.at[m, EXT - 16 : EXT - 16 + deep], row_s.at[a], row_r.at[a], {"sx": up})
        below = remote(ref.at[m, EXT - 16 - deep : EXT - 16], ref.at[m, 16 - deep : 16], row_s.at[b], row_r.at[b], {"sx": down})
        return [(above, has_up, has_down), (below, has_down, has_up)]

    def start_near(copies):
        for cp, sends, _ in copies:
            pl.when(sends)(cp.start)

    def await_near(copies):
        for cp, _, gets in copies:
            pl.when(gets)(cp.wait_recv)

    def main_copy(i, slot):
        start = jnp.clip(32 * i - 8, 0, ROWS - BLOCK)
        src = ce.at[:, pl.ds(pl.multiple_of(start + 16, 8), BLOCK)]
        dst = got.at[slot, :, pl.ds(pl.multiple_of(start + 16 - 32 * i, 8), BLOCK)]
        return remote(src, dst, a_s.at[i], a_r.at[slot], {"tm": 2 * i + p})

    def side_copy(side, i, slot):
        there = {"tm": 2 * i + p, "sy": (left, right)[side]}
        return remote(pt.at[side, i], gs.at[slot, side], h_s.at[side, i], h_r.at[slot, side], there)

    def edge_copy(low, slot):
        if low:
            there = {"tm": p, "sx": down}
            return remote(ce.at[:, EXT - 32 : EXT - 16], got.at[slot, :, 0:16], e_s.at[0], e_r.at[slot], there)
        there = {"tm": 2 * CHIPS - 2 + p, "sx": up}
        return remote(ce.at[:, 16:32], got.at[slot, :, 48:64], e_s.at[1], e_r.at[slot], there)

    def corner_copy(low, side, slot):
        there = {"tm": p, "sx": down} if low else {"tm": 2 * CHIPS - 2 + p, "sx": up}
        there["sy"] = (left, right)[side]
        src = pt.at[side, CHIPS if low else CHIPS + 1]
        return remote(src, gx.at[slot, side], k_s.at[2 * low + side], k_r.at[slot, side], there)

    def to_owners(act):
        for side, has in enumerate((has_left, has_right)):

            @pl.when(has)
            def _():
                def one(i, carry):
                    act(side_copy(side, i, c))
                    return carry

                lax.fori_loop(0, CHIPS, one, 0)

        for low, has in enumerate((has_up, has_down)):

            @pl.when(has)
            def _():
                act(edge_copy(low, c))

            for side, beside in enumerate((has_left, has_right)):

                @pl.when(has & beside)
                def _():
                    act(corner_copy(low, side, c))

    guess_near = strip_copies(0, 2, 3) + row_copies(2, ce, 8)
    other_near = strip_copies(1, 1, 2) + row_copies(1, ke)
    uses_initial = even | (c == 0)
    for cp, sends, gets in strip_copies(2, 0, 1) + row_copies(0, ie):
        other_near.append((cp, sends & uses_initial, gets & uses_initial))

    def send_main(d, carry):
        main_copy(lax.rem(c + d, CHIPS), c).start()
        return carry

    for cp in loads[2]:
        cp.wait()
    sp[0, 2] = pack(ce[0, 16 : 16 + ROWS], 0)
    sp[1, 2] = pack(ce[MAIN - 1, 16 : 16 + ROWS], 16)
    lane = lax.broadcasted_iota(jnp.int32, (8, 128), 1)
    none = jnp.zeros((8, 128), F32)
    for side in range(2):
        tiles = [none] + [sp[side, 2, k] for k in range(4)] + [none]
        for i in range(CHIPS):
            q, late = i // 2, i % 2
            back, cut = (96, 96) if late else (32, 32)
            a, b = pltpu.roll(tiles[q + late], back, 1), pltpu.roll(tiles[q + late + 1], back, 1)
            pt[side, i] = jnp.where(lane < cut, a, b)
        pt[side, CHIPS] = pltpu.roll(tiles[4], 32, 1)
        pt[side, CHIPS + 1] = pltpu.roll(tiles[1], 96, 1)
    for n, ref in ((0, ie), (1, ke)):
        for cp in loads[n]:
            cp.wait()
        sp[0, n] = pack(ref[0, 16 : 16 + ROWS], 0)
        sp[1, n] = pack(ref[MAIN - 1, 16 : 16 + ROWS], 16)
    pl.semaphore_wait(barrier, 2 * CHIPS - 1 + tall + broad + tall * broad + CHIPS * broad + tall + tall * broad)

    start_near(other_near + guess_near)

    @pl.when(sends_guess)
    def _():
        to_owners(lambda cp: cp.start())
        lax.fori_loop(1, CHIPS, send_main, 0)


    at = pl.multiple_of(32 * c, 32)
    start = jnp.clip(32 * c - 8, 0, ROWS - BLOCK)
    into = pl.ds(pl.multiple_of(start + 16 - 32 * c, 8), BLOCK)
    got[c, :, into] = ce[:, pl.ds(pl.multiple_of(start + 16, 8), BLOCK)]

    await_near(guess_near)

    mine = pl.multiple_of(8 + 128 * p, 8)

    def shift(h):
        to = {"tm": jnp.minimum(t + 1 + h, 2 * CHIPS - 1)}
        return [
            remote(ce.at[:, pl.ds(8 + 128 * h, HALF)], ph.at[0:MAIN], sh_s.at[2 * h], sh_r.at[0], to),
            remote(si.at[:, 2, pl.ds(2 * h, 4)], phs, sh_s.at[2 * h + 1], sh_r.at[1], to),
        ]

    own_even = [
        remote(ce.at[:, pl.ds(136, HALF)], qh.at[0:MAIN], eb_s.at[0], eb_r.at[0], {"tm": partner}),
        remote(si.at[:, 2, pl.ds(2, 4)], qhs, eb_s.at[1], eb_r.at[1], {"tm": partner}),
    ]

    @pl.when(even)
    def _():
        for cp in own_even:
            cp.start()

    await_near(other_near)
    unpack(ke, lambda side, k: si[side, 1, k], EXT // 8, 6)

    @pl.when(uses_initial)
    def _():
        unpack(ie, lambda side, k: si[side, 0, k], EXT // 8, 6)

    def window(m):
        @pl.when(m != c)
        def _():
            main_copy(c, m).wait_recv()

        pl.when(has_right)(lambda: side_copy(0, c, m).wait_recv())
        pl.when(has_left)(lambda: side_copy(1, c, m).wait_recv())
        outside = ((c == 0) & has_up) | ((c == CHIPS - 1) & has_down)

        @pl.when(outside)
        def _():
            edge_copy(1, m).wait_recv()

        @pl.when(outside & has_right)
        def _():
            corner_copy(1, 0, m).wait_recv()

        @pl.when(outside & has_left)
        def _():
            corner_copy(1, 1, m).wait_recv()

        outer = ((c == 0) & (lane < 32)) | ((c == CHIPS - 1) & (lane >= 96))
        r, l = (jnp.where(outer, gx[m, n], gs[m, n]) for n in range(2))
        side = jnp.concatenate([halo_rows(r, l, b) for b in range(8)], axis=0)
        return jnp.concatenate([got[m], side[None]], axis=0)

    def arrivals(count, act):
        def one(d, carry):
            m = lax.rem(c + CHIPS - d, CHIPS)

            @pl.when(m < count)
            def _():
                act(m)

            @pl.when(odd & (c < CHIPS - 1) & (d == 2))
            def _():
                for cp in shift(0) + shift(1):
                    cp.start()

            return carry

        lax.fori_loop(0, CHIPS, one, 0)

    def u_copy(m):
        return remote(us.at[m], ur.at[m + 1], u_s.at[m], u_r.at[m], {"tm": partner})

    half = c // 4

    def x_copy(i, j):
        dst = xb.at[:, pl.ds(pl.multiple_of(8 + 32 * lax.rem(i, 4), 8), 32)]
        return remote(xs.at[j, :, 16:48], dst, x_s.at[j], x_r.at[lax.rem(i, 4)], {"tm": 2 * j + i // 4})

    beyond = ((0, 8, 0, 0), (3, 40, 1, 0), (4, 16, 0, HALF - 8), (7, 48, 1, HALF - 8))

    def xe_copy(n, j):
        _, row, core, to = beyond[n]
        return remote(xs.at[j, :, row : row + 8], xb.at[:, to : to + 8], xe_s.at[j], xe_r.at[to // 128], {"tm": 2 * j + core})

    def for_x(j, act):
        @pl.when((j != c) | (half == 1))
        def _():
            act(x_copy(c, j))

        for n, (i, _, core, _) in enumerate(beyond):

            @pl.when((c == i) & ((j != i) | (core == 1)))
            def _():
                act(xe_copy(n, j))

    @pl.when(odd)
    def _():
        def point(m):
            us[m] = parts(window(m), ke[:, pl.ds(at, WIN)], work, True)[1]
            u_copy(m).start()

        arrivals(6, point)

    @pl.when(even)
    def _():
        kap0 = ke[:, pl.ds(at, WIN)]
        ur[0] = parts(ie[:, pl.ds(at, WIN)], kap0, work, True)[1]
        xs[0] = ie[:, pl.ds(at, WIN)]

        def ready(m):
            gp[m] = parts(window(m), ke[:, pl.ds(at, WIN)], work, False)

        arrivals(7, ready)

        def point(j, carry):
            @pl.when(j > 1)
            def _():
                u_copy(jnp.maximum(j - 2, 0)).wait_recv()

            x = xs[j - 1]
            xs[j] = x + 4.0 * lap(x, ke[:, pl.ds(at, WIN)], w2) + (ur[j - 1] + gp[j - 1])
            for_x(j, lambda cp: cp.start())

            @pl.when((j == c) & (half == 0))
            def _():
                xb[:, pl.ds(pl.multiple_of(8 + 32 * lax.rem(c, 4), 8), 32)] = xs[j, :, 16:48]

            @pl.when((j == c) & (c == 4))
            def _():
                xb[:, HALF - 8 : HALF] = xs[j, :, 16:24]

            return carry

        lax.fori_loop(1, CHIPS, point, 0)

    @pl.when(c == 0)
    def _():
        ph[...] = ie[:, pl.ds(mine, HALF)]
        xb[...] = ie[:, pl.ds(mine, HALF)]

    @pl.when(even)
    def _():
        qh[0:MAIN] = ce[:, 8 : 8 + HALF]
        unpack(qh, lambda side, k: si[side, 2, k], HALF // 8, 7)

    @pl.when(odd)
    def _():
        for cp in own_even:
            cp.wait_recv()
        unpack(qh, lambda side, k: qhs[side, k], HALF // 8, 7)

    @pl.when(c > 0)
    def _():
        for cp in shift(0):
            cp.wait_recv()
        unpack(ph, lambda side, k: phs[side, k], HALF // 8, 7)

    def ahead(b, carry):
        w = pl.ds(pl.multiple_of(32 * b, 32), BLOCK)
        kap = ke[:, pl.ds(pl.multiple_of(mine + 32 * b, 8), BLOCK)]
        g1, u = parts(ph[:, w], kap, work, True)
        ga[b] = g1
        gb[b] = u + parts(qh[:, w], kap, work, False)
        return carry

    lax.fori_loop(0, 4, ahead, 0)

    @pl.when(c > 0)
    def _():
        for k in range(4):

            @pl.when(odd | (c != k))
            def _():
                x_copy(k, c).wait_recv()

        xe_copy(0, c).wait_recv()

        @pl.when(odd | (c != 4))
        def _():
            xe_copy(2, c).wait_recv()

    def out_copy(b, n):
        o = pl.ds(pl.multiple_of(128 * p + 32 * b, 32), 32)
        src, dst = ((oc, c_out), (of, f_out))[n]
        return remote(src.at[b], dst.at[0, o], o_s.at[2 * b + n], o_r.at[2 * b + n], {"tm": partner})

    def finish(b, carry):
        w = pl.ds(pl.multiple_of(32 * b, 32), BLOCK)
        o = pl.ds(pl.multiple_of(128 * p + 32 * b, 32), 32)
        kap, x = ke[:, pl.ds(pl.multiple_of(mine + 32 * b, 8), BLOCK)], xb[:, w]
        lap_x = lap(x, kap, w0)
        mid = x + 2.0 * lap_x + ga[b]
        even_f = x + lap_x
        odd_c = x + 4.0 * lap_x + gb[b]
        odd_f = mid + lap(mid, kap, w1)

        def put(to_c, to_f, c_value, f_value):
            for k in range(MAIN):
                to_c[:, 128 * k : 128 * k + 128] = c_value[k, 8:40]
                to_f[:, 128 * k : 128 * k + 128] = f_value[k, 8:40]

        @pl.when(even)
        def _():
            put(oc.at[b], of.at[b], odd_c, odd_f)
            out_copy(b, 0).start()
            out_copy(b, 1).start()
            put(c_out.at[0, o], f_out.at[0, o], mid, even_f)

        @pl.when(odd)
        def _():
            put(oc.at[b], of.at[b], mid, even_f)
            out_copy(b, 0).start()
            out_copy(b, 1).start()
            put(c_out.at[0, o], f_out.at[0, o], odd_c, odd_f)

        return carry

    lax.fori_loop(0, 4, finish, 0)

    for cp, sends, _ in guess_near + other_near:
        pl.when(sends)(cp.wait_send)

    @pl.when(sends_guess)
    def _():
        def sent(d, carry):
            main_copy(lax.rem(c + d, CHIPS), c).wait_send()
            return carry

        lax.fori_loop(1, CHIPS, sent, 0)
        to_owners(lambda cp: cp.wait_send())

    @pl.when(odd)
    def _():
        @pl.when(c < CHIPS - 1)
        def _():
            for cp in shift(0) + shift(1):
                cp.wait_send()

        def sent(m, carry):
            u_copy(m).wait_send()
            return carry

        lax.fori_loop(0, 6, sent, 0)

    @pl.when(even)
    def _():
        for cp in own_even:
            cp.wait_send()

        def sent(j, carry):
            for_x(j, lambda cp: cp.wait_send())
            return carry

        lax.fori_loop(1, CHIPS, sent, 0)

    def landed(b, carry):
        for n in range(2):
            out_copy(b, n).wait()
        return carry

    lax.fori_loop(0, 4, landed, 0)


def store(c_ref, f_ref, c_hbm, f_hbm, sem):
    copies = [pltpu.make_async_copy(src, dst, sem.at[n]) for n, (src, dst) in enumerate(((c_ref, c_hbm), (f_ref, f_hbm)))]
    for cp in copies:
        cp.start()
    for cp in copies:
        cp.wait()


def solution(mesh):
    def dma(*shape):
        return pltpu.SemaphoreType.DMA(shape) if shape else pltpu.SemaphoreType.DMA

    def vmem(*shape):
        return pltpu.VMEM(shape, F32)

    def on_device(initial, kappa, guess):
        tile = jax.ShapeDtypeStruct((1, ROWS, COLS), F32)
        c, f = pl.pallas_call(
            kernel,
            out_shape=(tile, tile),
            in_specs=[pl.BlockSpec(memory_space=pltpu.HBM)] * 3,
            out_specs=(pl.BlockSpec(memory_space=pltpu.VMEM),) * 2,
            scratch_shapes=[
                vmem(WIDE, EXT, 128), vmem(WIDE, EXT, 128), vmem(MAIN, EXT, 128),
                vmem(2, 3, 4, 8, 128), vmem(2, 3, 6, 8, 128), vmem(2, CHIPS + 2, 8, 128),
                vmem(CHIPS, 2, 8, 128), vmem(CHIPS, 2, 8, 128),
                vmem(CHIPS, MAIN, WIN, 128), vmem(7, WIDE, WIN, 128), vmem(6, WIDE, WIN, 128), vmem(7, WIDE, WIN, 128), vmem(8, WIDE, WIN, 128),
                vmem(WIDE, HALF, 128), vmem(WIDE, HALF, 128), vmem(2, 4, 8, 128), vmem(WIDE, HALF, 128), vmem(2, 4, 8, 128),
                vmem(4, WIDE, BLOCK, 128), vmem(4, WIDE, BLOCK, 128), vmem(4, 32, COLS), vmem(4, 32, COLS),
                vmem(WIDE, WIN + 16, 128), vmem(WIDE, WIN + 16, 128), vmem(WIDE, WIN + 16, 128),
                dma(12), dma(6), dma(6), dma(12), dma(12), dma(6), dma(6),
                dma(8), dma(8), dma(2, 8), dma(8, 2), dma(2), dma(8), dma(4), dma(8, 2), dma(4), dma(2), dma(2), dma(2),
                dma(6), dma(6), dma(8), dma(4), dma(8), dma(2), dma(8), dma(8),
            ],
            compiler_params=pltpu.CompilerParams(
                collective_id=0, has_side_effects=True, vmem_limit_bytes=32 * 2**20
            ),
        )(*(pltpu.with_memory_space_constraint(x, pltpu.HBM) for x in (initial, kappa, guess)))
        return pl.pallas_call(
            store,
            out_shape=(tile, tile),
            in_specs=[pl.BlockSpec(memory_space=pltpu.VMEM)] * 2,
            out_specs=(pl.BlockSpec(memory_space=pltpu.HBM),) * 2,
            scratch_shapes=[dma(2)],
            compiler_params=pltpu.CompilerParams(vmem_limit_bytes=16 * 2**20),
        )(c, f)

    return jax.shard_map(
        on_device,
        mesh=mesh,
        in_specs=(P("sx", "sy"), P("sx", "sy"), P("tm", "sx", "sy")),
        out_specs=(P("tm", "sx", "sy"), P("tm", "sx", "sy")),
        check_vma=False,
    )
```
